512 devices in a mesh: seq: 64 (over z_hi, y, core), grp: 8 (over x, z_lo).
Axes of the slice: x: 4, y: 8, z: 8 (z_hi: 4, z_lo: 2; z = z_hi * 2 + z_lo), core: 2. Of those that a mesh axis runs over, the one named last changes fastest.
Arguments:
- embeddings: bfloat16 [1536, 32768], P('grp', 'seq'), may hold values from -6 to 6
- hilbert_order: int32 [32768], P('seq'), may hold values from 0 to 32767, as said below
- cotangent: bfloat16 [1536, 32768], P('grp', 'seq'), may hold values from -6 to 6
- first_conv_weight: bfloat16 [8, 110592], P('grp'), may hold values from -0.25 to 0.25
- first_pointwise_weight: bfloat16 [1536, 1536], P('grp'), may hold values from -0.21875 to 0.21875
- second_conv_weight: bfloat16 [8, 110592], P('grp'), may hold values from -0.25 to 0.25
- second_pointwise_weight: bfloat16 [1536, 1536], P('grp'), may hold values from -0.21875 to 0.21875
Outputs:
- emb_grad: bfloat16 [1536, 32768], P('grp', 'seq')
- first_conv_gradient: bfloat16 [8, 110592], P('grp')
- first_pointwise_gradient: bfloat16 [1536, 1536], P('grp')
- second_conv_gradient: bfloat16 [8, 110592], P('grp')
- second_pointwise_gradient: bfloat16 [1536, 1536], P('grp')
The draws below stay inside these ranges and needn't reach their ends.
Inputs may be any that keep to these rules, and one draw needn't show every extreme that they name: `hilbert_order`: every aligned block of 512 positions holds each patch index of that same block exactly once.
All inputs are finite; a program needn't handle non-finite values.
Results may differ from the reference program's by a relative error of at most 0.018.
Values may be sent and summed in bfloat16 or wider, within the bound.
No kernel may reach another device: no remote copies, remote signals or barrier semaphores. Data moves between devices by JAX's collectives and lax.ppermute only.
A program may use at most 64 MiB of HBM per device.

```python
import jax
import jax.numpy as jnp
from jax import lax

D = 1536
GROUPS = 8
TOK_DEV = 512
CG = 192
TOKENS = 32768
DILATION_FIRST = 2048
DILATION_SECOND = 4096
N_GRP = 8


def draw_hilbert_order(key, part):
    blocks = TOKENS // TOK_DEV
    block_keys = jax.random.split(jax.random.fold_in(key, 11), blocks)
    orders = jax.vmap(lambda block_key: jax.random.permutation(block_key, TOK_DEV))(block_keys)
    offsets = jnp.arange(blocks, dtype=jnp.int32)[:, None] * TOK_DEV
    return (orders.astype(jnp.int32) + offsets).reshape(TOKENS)


def raised(values, rng, source, target, blocks, factor):
    def block_of(position):
        return (jnp.arange(values.shape[position]) // (values.shape[position] // blocks)).reshape((-1,) + (1,) * (values.ndim - 1 - position))

    one_side = jax.random.permutation(rng, blocks)[block_of(target)]
    second = (block_of(target) + blocks // 2) % blocks
    return jnp.where((block_of(source) == one_side) | (block_of(source) == second), factor * values, values)


def level_of(own_key, extent, cuts, smallest, largest):
    level, own = 1.0, jax.random.fold_in(own_key, 6)
    for position, parts in cuts:
        steps = jnp.exp(jax.random.uniform(jax.random.fold_in(own, position), (parts,), jnp.float32, smallest / len(cuts), largest / len(cuts)))
        level = level * jnp.repeat(steps, extent[position] // parts).reshape([-1 if axis == position else 1 for axis in range(len(extent))])
    return level


def scatter_about(stream_key, dims, spread, limit, cuts=(), held_as=jnp.bfloat16):
    entries = spread * jax.random.normal(stream_key, dims, jnp.float32)
    if cuts:
        entries = entries * level_of(stream_key, dims, cuts, -0.22, 0.18)
    return jnp.clip(entries, -limit, limit).astype(held_as)


def heavy_noise(rng, dims, spread, reach, cuts, heavy, held_as=jnp.bfloat16):
    values = spread * jax.random.normal(rng, dims, jnp.float32)
    if cuts:
        values = values * level_of(rng, dims, cuts, -0.22, 0.18)
    return jnp.clip(raised(values, jax.random.fold_in(rng, 3), *heavy), -reach, reach).astype(held_as)


def setup_inputs(seed: int = 0) -> dict:
    seeds = jax.random.split(jax.random.key(seed), 8)
    embeddings = scatter_about(seeds[0], (D, TOKENS), 1.0, 6.0, ((0, 8), (1, 64)))
    hilbert_order = draw_hilbert_order(jax.random.fold_in(seeds[7], 71), 0)
    cotangent = scatter_about(seeds[2], (D, TOKENS), 1.0, 6.0, ((0, 8), (1, 64)))
    first_conv_weight = scatter_about(seeds[3], (GROUPS, 3 * CG * CG), (3 * CG) ** -0.5, 0.25, ((0, 8),))
    first_pointwise_weight = heavy_noise(seeds[4], (D, D), D ** -0.5, 0.21875, ((0, 8),), (0, 1, 8, 2.0))
    second_conv_weight = scatter_about(seeds[5], (GROUPS, 3 * CG * CG), (3 * CG) ** -0.5, 0.25, ((0, 8),))
    second_pointwise_weight = heavy_noise(seeds[6], (D, D), D ** -0.5, 0.21875, ((0, 8),), (0, 1, 8, 2.0))
    return dict(embeddings=embeddings, hilbert_order=hilbert_order, cotangent=cotangent, first_conv_weight=first_conv_weight, first_pointwise_weight=first_pointwise_weight, second_conv_weight=second_conv_weight, second_pointwise_weight=second_pointwise_weight)


def before_cols(values, dilation):
    filler = jnp.zeros((values.shape[0], dilation), values.dtype)
    return jnp.concatenate([filler, values[:, :-dilation]], axis=1)

def after_cols(values, dilation):
    filler = jnp.zeros((values.shape[0], dilation), values.dtype)
    return jnp.concatenate([values[:, dilation:], filler], axis=1)

def tap_weights(conv_weight, tap):
    return conv_weight.astype(jnp.float32).reshape(GROUPS, 3, CG, CG)[:, tap]

def group_apply(values, weight_tap):
    col_count = values.shape[1]
    grouped = values.astype(jnp.float32).reshape(GROUPS, CG, col_count)
    return jnp.einsum('git,gio->got', grouped, weight_tap).reshape(D, col_count)

def group_back(grads, weight_tap):
    col_count = grads.shape[1]
    grouped = grads.astype(jnp.float32).reshape(GROUPS, CG, col_count)
    return jnp.einsum('got,gio->git', grouped, weight_tap).reshape(D, col_count)

def group_grad(values, grads):
    col_count = values.shape[1]
    grouped = values.astype(jnp.float32).reshape(GROUPS, CG, col_count)
    grad_grouped = grads.astype(jnp.float32).reshape(GROUPS, CG, col_count)
    return jnp.einsum('git,got->gio', grouped, grad_grouped)

def block_forward_step(inputs, conv_weight, dilation):
    tap_set = (before_cols(inputs, dilation), inputs, after_cols(inputs, dilation))
    hidden = group_apply(tap_set[0], tap_weights(conv_weight, 0)) + group_apply(tap_set[1], tap_weights(conv_weight, 1)) + group_apply(tap_set[2], tap_weights(conv_weight, 2))
    activated = jax.nn.silu(hidden).astype(jnp.bfloat16)
    return (tap_set, hidden, activated)

def block_backward_step(grad_out, tap_set, hidden, activated, conv_weight, pointwise, dilation, gradient_scale):
    point_grad = lax.dot_general(grad_out, activated, (((1,), (1,)), ((), ())), preferred_element_type=jnp.float32) * gradient_scale
    shard_width = D // N_GRP
    grad_hidden = jnp.zeros((D, grad_out.shape[1]), jnp.float32)
    for shard_index in range(N_GRP):
        lowest = shard_index * shard_width
        partial_sum = lax.dot_general(pointwise[lowest:lowest + shard_width], grad_out[lowest:lowest + shard_width], (((0,), (0,)), ((), ())), preferred_element_type=jnp.float32)
        rounded = lax.optimization_barrier(partial_sum.astype(jnp.bfloat16))
        grad_hidden = grad_hidden + rounded.astype(jnp.float32)
    sigmoid_h = jax.nn.sigmoid(hidden)
    grad_pre = (grad_hidden * sigmoid_h * (1.0 + hidden * (1.0 - sigmoid_h))).astype(jnp.bfloat16)
    conv_grad = jnp.stack([group_grad(tap_values, grad_pre) for tap_values in tap_set], axis=1).reshape(GROUPS, 3 * CG * CG) * gradient_scale
    grad_taps = (after_cols(grad_pre, dilation), grad_pre, before_cols(grad_pre, dilation))
    grad_input = grad_out.astype(jnp.float32) + group_back(grad_taps[0], tap_weights(conv_weight, 0)) + group_back(grad_taps[1], tap_weights(conv_weight, 1)) + group_back(grad_taps[2], tap_weights(conv_weight, 2))
    return (grad_input.astype(jnp.bfloat16), conv_grad.astype(jnp.bfloat16), point_grad.astype(jnp.bfloat16))

def reference(embeddings, hilbert_order, cotangent, first_conv_weight, first_pointwise_weight, second_conv_weight, second_pointwise_weight):
    gradient_scale = float(TOKENS) ** (-0.5)
    initial_token_rows = jnp.take(embeddings, hilbert_order, axis=1)
    first_tap_rows, first_hidden_state, first_activation_output = block_forward_step(initial_token_rows, first_conv_weight, DILATION_FIRST)
    middle_rows = (initial_token_rows.astype(jnp.float32) + jnp.dot(first_pointwise_weight, first_activation_output, preferred_element_type=jnp.float32)).astype(jnp.bfloat16)
    second_tap_rows, second_hidden_state, second_activation_output = block_forward_step(middle_rows, second_conv_weight, DILATION_SECOND)
    middle_gradient, second_conv_gradient, second_pointwise_gradient = block_backward_step(cotangent, second_tap_rows, second_hidden_state, second_activation_output, second_conv_weight, second_pointwise_weight, DILATION_SECOND, gradient_scale)
    start_gradient, first_conv_gradient, first_pointwise_gradient = block_backward_step(middle_gradient, first_tap_rows, first_hidden_state, first_activation_output, first_conv_weight, first_pointwise_weight, DILATION_FIRST, gradient_scale)
    emb_grad = jnp.zeros_like(start_gradient).at[:, hilbert_order].set(start_gradient)
    return (emb_grad, first_conv_gradient, first_pointwise_gradient, second_conv_gradient, second_pointwise_gradient)
```

```python
import jax
import jax.numpy as jnp
from jax import lax
from jax.sharding import Mesh, PartitionSpec as P

CG = 192
BF = jnp.bfloat16
F32 = jnp.float32
SEQ = ("zh", "yh", "yl", "core")
GRP = ("x", "zl")
SAME = ("zh", "yh")
CHIPS = ("zh", "yh", "yl")


def mm(a, b, ca, cb):
    return lax.dot_general(a, b, (((ca,), (cb,)), ((), ())), preferred_element_type=F32)


def swap(blocks, axes):
    return lax.all_to_all(blocks, axes, 0, 0, tiled=True)


def shifted(values, by):
    rows, cols = values.shape
    if by == 0:
        return values
    filler = jnp.zeros((rows, abs(by)), values.dtype)
    if by > 0:
        return jnp.concatenate([values[:, by:], filler], axis=1)
    return jnp.concatenate([filler, values[:, :by]], axis=1)


def taps(values, by):
    return (shifted(values, -by), values, shifted(values, by))


def conv(values, weight, by):
    return sum(mm(weight[k], tap, 0, 0) for k, tap in enumerate(taps(values, by)))


def conv_back(grads, weight, by):
    return sum(mm(weight[k], tap, 1, 0) for k, tap in enumerate(taps(grads, by)[::-1]))


def conv_grad(values, grads, by):
    return jnp.concatenate([mm(tap, grads, 1, 1) for tap in taps(values, by)], axis=0)


def other_core(values):
    return lax.ppermute(values, "core", [(0, 1), (1, 0)])


def core_sum(partial):
    first = lax.axis_index("core") == 0
    mine = jnp.where(first, partial[0], partial[1])
    got = other_core(jnp.where(first, partial[1], partial[0]))
    return (mine.astype(F32) + got.astype(F32)).astype(BF)


def chips_sum(half, scale):
    return (jnp.sum(swap(half, CHIPS).astype(F32), axis=0) * scale).astype(BF)


def chips_spread(piece):
    everyone = swap(jnp.broadcast_to(piece[None], (32,) + piece.shape), CHIPS)
    other = other_core(everyone)
    first = lax.axis_index("core") == 0
    return jnp.concatenate([jnp.where(first, everyone, other), jnp.where(first, other, everyone)], axis=0)


def conv_rows(grad):
    rows = grad.astype(BF).reshape(864, 128)
    return jnp.pad(rows, ((0, 32), (0, 0))).reshape(2, 32, 14, 128)


def conv_flat(rows):
    return rows.reshape(896 * 128)[: 3 * CG * CG].reshape(1, 3 * CG * CG)


def local(emb, order, cot, cw1, pw1, cw2, pw2):
    scale = float(32768) ** (-0.5)
    cols = emb.shape[1]
    s = lax.axis_index(SEQ)
    index = order - s * cols
    w1 = cw1.reshape(3, CG, CG)
    w2 = cw2.reshape(3, CG, CG)
    onehot = (lax.broadcasted_iota(jnp.int32, (cols, cols), 0) == index[None, :]).astype(BF)
    eye = (
        lax.broadcasted_iota(jnp.int32, (CG, CG), 0) == lax.broadcasted_iota(jnp.int32, (CG, CG), 1)
    ).astype(BF)
    start_t = mm(onehot, emb, 0, 1).astype(BF)
    packed = jnp.concatenate([start_t, cot.T], axis=1).reshape(16, cols // 16, 2 * CG)
    packed = swap(packed, SAME).reshape(cols, 2 * CG)
    start = mm(eye, packed[:, :CG], 1, 1).astype(BF)
    cotq = mm(eye, packed[:, CG:], 1, 1).astype(BF)

    near_hidden = conv(start, w1, 32)
    near_act = jax.nn.silu(near_hidden).astype(BF)
    act_all = swap(jnp.broadcast_to(near_act[None], (8, CG, cols)), GRP).reshape(8 * CG, cols)

    pw2_blocks = pw2.reshape(CG, 8, CG).transpose(1, 0, 2)
    sent = jnp.concatenate([jnp.broadcast_to(cotq[None], (8, CG, cols)), pw2_blocks], axis=2)
    sent = swap(sent, GRP).reshape(8 * CG, cols + CG)
    cot_all, pw2_cols = sent[:, :cols], sent[:, cols:]

    middle = (start.astype(F32) + mm(pw1, act_all, 1, 0)).astype(BF)
    far_hidden = conv(middle, w2, 64)
    far_s = jax.nn.sigmoid(far_hidden)
    far_act = (far_hidden * far_s).astype(BF)
    far_da = mm(pw2_cols, cot_all, 0, 0)
    far_dh = (far_da * far_s * (1.0 + far_hidden * (1.0 - far_s))).astype(BF)
    grad_middle = (cotq.astype(F32) + conv_back(far_dh, w2, 64)).astype(BF)

    parts = mm(pw1, grad_middle, 0, 0).astype(BF).reshape(8, CG, cols)
    got = swap(parts, GRP)
    near_da = jnp.sum(got.astype(F32), axis=0)

    pg2 = mm(cot_all, far_act, 1, 1).astype(BF)
    pg2 = pg2.reshape(8, 2, 32, 3 * CG).transpose(1, 2, 0, 3).reshape(2, 32, 36, 128)
    pg1 = mm(grad_middle, act_all, 1, 1).astype(BF).reshape(2, 32, 36, 128)
    cg2 = conv_rows(conv_grad(middle, far_dh, 64))
    early = chips_sum(core_sum(jnp.concatenate([pg1, pg2, cg2], axis=2)), scale)
    piece2 = swap(early[36:72].reshape(8, 3 * CG), GRP)
    piece2 = piece2.reshape(8, 3, CG).transpose(1, 0, 2).reshape(36, 128)

    near_s = jax.nn.sigmoid(near_hidden)
    near_dh = (near_da * near_s * (1.0 + near_hidden * (1.0 - near_s))).astype(BF)
    grad_start = (grad_middle.astype(F32) + conv_back(near_dh, w1, 32)).astype(BF)
    cg1 = conv_rows(conv_grad(start, near_dh, 32))
    late = chips_sum(core_sum(cg1), scale)
    whole = chips_spread(jnp.concatenate([early[:36], piece2, early[72:], late], axis=0))
    out_pg1 = whole[:, :36].reshape(CG, 8 * CG)
    out_pg2 = whole[:, 36:72].reshape(CG, 8 * CG)
    out_cg2 = conv_flat(whole[:, 72:86])
    out_cg1 = conv_flat(whole[:, 86:])

    back = mm(grad_start, eye, 0, 0).astype(BF).reshape(16, cols // 16, CG)
    back = swap(back, SAME).reshape(cols, CG)
    emb_grad = mm(back, onehot, 0, 1).astype(BF)
    return emb_grad, out_cg1, out_pg1, out_cg2, out_pg2


def solution(mesh):
    fine = Mesh(mesh.devices.reshape(4, 4, 2, 2, 4, 2), SEQ + GRP)
    placed = (P(GRP, SEQ), P(SEQ), P(GRP, SEQ), P(GRP, None), P(GRP, None), P(GRP, None), P(GRP, None))
    return jax.shard_map(
        local,
        mesh=fine,
        in_specs=placed,
        out_specs=(P(GRP, SEQ), P(GRP, None), P(GRP, None), P(GRP, None), P(GRP, None)),
        check_vma=False,
    )
```

```python
import jax
import jax.numpy as jnp
from jax import lax
from jax.sharding import Mesh, PartitionSpec as P

CG = 192
BF = jnp.bfloat16
F32 = jnp.float32
SEQ = ("zh", "yh", "yl", "core")
GRP = ("x", "zl")
CHIPS = ("zh", "yh", "yl")


def mm(a, b, ca, cb):
    return lax.dot_general(a, b, (((ca,), (cb,)), ((), ())), preferred_element_type=F32)


def swap(blocks, axes):
    return lax.all_to_all(blocks, axes, 0, 0, tiled=True)


def shifted(values, by):
    rows, cols = values.shape
    if by == 0:
        return values
    filler = jnp.zeros((rows, abs(by)), values.dtype)
    if by > 0:
        return jnp.concatenate([values[:, by:], filler], axis=1)
    return jnp.concatenate([filler, values[:, :by]], axis=1)


def taps(values, by):
    return (shifted(values, -by), values, shifted(values, by))


def conv(values, weight, by):
    return sum(mm(weight[k], tap, 0, 0) for k, tap in enumerate(taps(values, by)))


def conv_back(grads, weight, by):
    return sum(mm(weight[k], tap, 1, 0) for k, tap in enumerate(taps(grads, by)[::-1]))


def conv_grad(values, grads, by):
    return jnp.concatenate([mm(tap, grads, 1, 1) for tap in taps(values, by)], axis=0)


def other_core(values):
    return lax.ppermute(values, "core", [(0, 1), (1, 0)])


def core_sum(partial):
    first = lax.axis_index("core") == 0
    mine = jnp.where(first, partial[0], partial[1])
    got = other_core(jnp.where(first, partial[1], partial[0]))
    return (mine.astype(F32) + got.astype(F32)).astype(BF)


def conv_rows(grad):
    rows = grad.astype(BF).reshape(864, 128)
    return jnp.pad(rows, ((0, 32), (0, 0))).reshape(2, 32, 14, 128)


def conv_flat(rows):
    return rows.reshape(896 * 128)[: 3 * CG * CG].reshape(1, 3 * CG * CG)


def local(emb, order, cot, cw1, pw1, cw2, pw2):
    scale = float(32768) ** (-0.5)
    cols = emb.shape[1]
    s = lax.axis_index(SEQ)
    index = order - s * cols
    w1 = cw1.reshape(3, CG, CG)
    w2 = cw2.reshape(3, CG, CG)
    onehot = (lax.broadcasted_iota(jnp.int32, (cols, cols), 0) == index[None, :]).astype(BF)
    eye = (
        lax.broadcasted_iota(jnp.int32, (CG, CG), 0) == lax.broadcasted_iota(jnp.int32, (CG, CG), 1)
    ).astype(BF)
    start_t = mm(onehot, emb, 0, 1).astype(BF)
    packed = jnp.concatenate([start_t, cot.T], axis=1).reshape(32, cols // 32, 2 * CG)
    packed = swap(packed, CHIPS).reshape(cols, 2 * CG)
    start = mm(eye, packed[:, :CG], 1, 1).astype(BF)
    cotq = mm(eye, packed[:, CG:], 1, 1).astype(BF)

    near_hidden = conv(start, w1, 32)
    near_act = jax.nn.silu(near_hidden).astype(BF)
    act_all = swap(jnp.broadcast_to(near_act[None], (8, CG, cols)), GRP).reshape(8 * CG, cols)

    pw2_blocks = pw2.reshape(CG, 8, CG).transpose(1, 0, 2)
    sent = jnp.concatenate([jnp.broadcast_to(cotq[None], (8, CG, cols)), pw2_blocks], axis=2)
    sent = swap(sent, GRP).reshape(8 * CG, cols + CG)
    cot_all, pw2_cols = sent[:, :cols], sent[:, cols:]

    middle = (start.astype(F32) + mm(pw1, act_all, 1, 0)).astype(BF)
    far_hidden = conv(middle, w2, 64)
    far_s = jax.nn.sigmoid(far_hidden)
    far_act = (far_hidden * far_s).astype(BF)
    far_da = mm(pw2_cols, cot_all, 0, 0)
    far_dh = (far_da * far_s * (1.0 + far_hidden * (1.0 - far_s))).astype(BF)
    grad_middle = (cotq.astype(F32) + conv_back(far_dh, w2, 64)).astype(BF)

    parts = mm(pw1, grad_middle, 0, 0).astype(BF).reshape(8, CG, cols)
    got = swap(parts, GRP)
    near_da = jnp.sum(got.astype(F32), axis=0)

    pg2 = mm(cot_all, far_act, 1, 1).astype(BF)
    pg2 = pg2.reshape(8, 2, 32, 3 * CG).transpose(1, 2, 0, 3).reshape(2, 32, 36, 128)
    pg1 = mm(grad_middle, act_all, 1, 1).astype(BF).reshape(2, 32, 36, 128)
    cg2 = conv_rows(conv_grad(middle, far_dh, 64))
    early = core_sum(jnp.concatenate([pg1, pg2, cg2], axis=2))

    near_s = jax.nn.sigmoid(near_hidden)
    near_dh = (near_da * near_s * (1.0 + near_hidden * (1.0 - near_s))).astype(BF)
    grad_start = (grad_middle.astype(F32) + conv_back(near_dh, w1, 32)).astype(BF)
    cg1 = conv_rows(conv_grad(start, near_dh, 32))
    late = core_sum(cg1)
    back = mm(grad_start, eye, 0, 0).astype(BF).reshape(32, cols * CG // 32 // 128, 128)
    got = swap(jnp.concatenate([early, late, back], axis=1), CHIPS)
    piece = (jnp.sum(got[:, :100].astype(F32), axis=0) * scale).astype(BF)
    piece2 = swap(piece[36:72].reshape(8, 3 * CG), GRP)
    piece2 = piece2.reshape(8, 3, CG).transpose(1, 0, 2).reshape(36, 128)
    piece = jnp.concatenate([piece[:36], piece2, piece[72:]], axis=0)
    everyone = swap(jnp.broadcast_to(piece[None], (32, 100, 128)), CHIPS)
    other = other_core(everyone)
    first = lax.axis_index("core") == 0
    whole = jnp.concatenate([jnp.where(first, everyone, other), jnp.where(first, other, everyone)], axis=0)
    out_pg1 = whole[:, :36].reshape(CG, 8 * CG)
    out_pg2 = whole[:, 36:72].reshape(CG, 8 * CG)
    out_cg2 = conv_flat(whole[:, 72:86])
    out_cg1 = conv_flat(whole[:, 86:])
    emb_grad = mm(got[:, 100:].reshape(cols, CG), onehot, 0, 1).astype(BF)
    return emb_grad, out_cg1, out_pg1, out_cg2, out_pg2


def solution(mesh):
    fine = Mesh(mesh.devices.reshape(4, 4, 2, 2, 4, 2), SEQ + GRP)
    placed = (P(GRP, SEQ), P(SEQ), P(GRP, SEQ), P(GRP, None), P(GRP, None), P(GRP, None), P(GRP, None))
    return jax.shard_map(
        local,
        mesh=fine,
        in_specs=placed,
        out_specs=(P(GRP, SEQ), P(GRP, None), P(GRP, None), P(GRP, None), P(GRP, None)),
        check_vma=False,
    )
```

```python
import jax
import jax.numpy as jnp
from jax import lax
from jax.experimental import pallas as pl
from jax.experimental.pallas import tpu as pltpu
from jax.sharding import Mesh, PartitionSpec as P

CG = 192
TOK = 512
NEAR = 32
FAR = 64
BF = jnp.bfloat16
F32 = jnp.float32
SEQ = ("zh", "yh", "yl", "core")
GRP = ("x", "zl")
CHIPS = ("zh", "yh", "yl")
SCALE = float(32768) ** (-0.5)
ROWS = 104


def mm(a, b, ca, cb):
    return lax.dot_general(a, b, (((ca,), (cb,)), ((), ())), preferred_element_type=F32)


def swap(blocks, axes):
    return lax.all_to_all(blocks, axes, 0, 0, tiled=True)


def other_core(values):
    return lax.ppermute(values, "core", [(0, 1), (1, 0)])


def call(kernel, outs, scalars, *arrays, scratch=()):
    vmem = pl.BlockSpec(memory_space=pltpu.VMEM)
    smem = pl.BlockSpec(memory_space=pltpu.SMEM)
    return pl.pallas_call(
        kernel,
        out_shape=[jax.ShapeDtypeStruct(shape, dtype) for shape, dtype in outs],
        in_specs=[smem] * len(scalars) + [vmem] * len(arrays),
        out_specs=[vmem] * len(outs),
        scratch_shapes=[pltpu.VMEM(shape, dtype) for shape, dtype in scratch],
        compiler_params=pltpu.CompilerParams(vmem_limit_bytes=48 * 1024 * 1024),
    )(*scalars, *arrays)


def shifted(values, by):
    if by == 0:
        return values.astype(BF)
    lane = lax.broadcasted_iota(jnp.int32, values.shape, 1)
    rolled = pltpu.roll(values, (-by) % TOK, 1)
    keep = lane < TOK - by if by > 0 else lane >= -by
    return jnp.where(keep, rolled, 0.0).astype(BF)


def conv_back(grads, weight_ref, by):
    return (
        mm(weight_ref[0], shifted(grads, by), 1, 0)
        + mm(weight_ref[1], shifted(grads, 0), 1, 0)
        + mm(weight_ref[2], shifted(grads, -by), 1, 0)
    )


def conv_rows(values, grads, by, rows_ref):
    row = lax.broadcasted_iota(jnp.int32, (CG, CG), 0)
    col = lax.broadcasted_iota(jnp.int32, (CG, CG), 1)
    half = CG // 2
    source = jnp.where(row < half, 2 * row, 2 * row - (CG - 1))
    order = jnp.where(col == source, 1.0, 0.0).astype(BF)
    for tap, distance in enumerate((-by, 0, by)):
        moved = mm(order, shifted(values, distance), 1, 0).astype(BF)
        grad = mm(moved, grads, 1, 1)
        even, odd = grad[:half], grad[half:]
        base = 3 * half * tap
        rows_ref[base : base + half] = even[:, :128]
        rows_ref[base + half : base + 2 * half] = jnp.concatenate([even[:, 128:], odd[:, :64]], axis=1)
        rows_ref[base + 2 * half : base + 3 * half] = odd[:, 64:]


def pack_kernel(base_ref, order_ref, emb_ref, cot_ref, out_ref):
    token = lax.broadcasted_iota(jnp.int32, (TOK, TOK), 0)
    onehot = jnp.where(token == order_ref[...] - base_ref[0], 1.0, 0.0).astype(BF)
    start = mm(emb_ref[...], onehot, 1, 0)
    both = jnp.concatenate([start, cot_ref[...].astype(F32)], axis=0)
    out_ref[...] = both.T.astype(BF)


def near_kernel(tokens_ref, weight_ref, act_ref, hidden_ref, start_ref, cot_ref):
    rows = tokens_ref[...].astype(F32)
    both = rows.T
    start_ref[...] = both[:CG].astype(BF)
    cot_ref[...] = both[CG:].astype(BF)
    start = rows[:, :CG]
    filler = jnp.zeros((NEAR, CG), F32)
    before = jnp.concatenate([filler, start[: TOK - NEAR]], axis=0).astype(BF)
    after = jnp.concatenate([start[NEAR:], filler], axis=0).astype(BF)
    hidden = (
        mm(weight_ref[0], before, 1, 1)
        + mm(weight_ref[1], start.astype(BF), 1, 1)
        + mm(weight_ref[2], after, 1, 1)
    )
    hidden_ref[...] = hidden
    act = (hidden * jax.nn.sigmoid(hidden)).astype(BF)
    for j in range(8):
        act_ref[j] = act


def regroup_kernel(core_ref, sent_ref, act_ref, mine_ref, other_ref, grad_ref):
    for j in range(8):
        grad_ref[j * CG : (j + 1) * CG] = mm(sent_ref[j, :, :TOK], act_ref[...], 1, 1)
    blank = jnp.zeros((8, 64), F32)
    for out_ref, core in ((mine_ref, core_ref[0]), (other_ref, 1 - core_ref[0])):
        for j in range(8):
            for part in range(4):
                piece = grad_ref[pl.ds(pl.multiple_of(j * CG + 96 * core + 24 * part, 8), 24)]
                rest = piece[:, 128:]
                at = 40 * part
                out_ref[j, at : at + 24] = piece[:, :128].astype(out_ref.dtype)
                out_ref[j, at + 24 : at + 32] = jnp.concatenate([rest[:8], rest[8:16]], axis=1).astype(out_ref.dtype)
                out_ref[j, at + 32 : at + 40] = jnp.concatenate([rest[16:], blank], axis=1).astype(out_ref.dtype)


def far_kernel(sent_ref, hidden_ref, cot_ref, weight_ref, dh_ref, grad_ref):
    da = sum(mm(sent_ref[j, :, TOK:], sent_ref[j, :, :TOK], 0, 0) for j in range(8))
    hidden = hidden_ref[...]
    s = jax.nn.sigmoid(hidden)
    dh = (da * s * (1.0 + hidden * (1.0 - s))).astype(BF)
    dh_ref[...] = dh
    back = conv_back(dh.astype(F32), weight_ref, FAR)
    grad_ref[...] = (cot_ref[...].astype(F32) + back).astype(BF)


def parts_kernel(grad_ref, pointwise_ref, mine_ref, other_ref, out_ref):
    grad = grad_ref[...]
    for j in range(8):
        out_ref[j, :, :TOK] = mm(pointwise_ref[j * CG : (j + 1) * CG], grad, 1, 0).astype(BF)
        out_ref[j, :160, TOK:] = (mine_ref[j] + other_ref[j].astype(F32)).astype(BF)
        out_ref[j, 160:, TOK:] = jnp.zeros((32, 128), BF)


def early_kernel(core_ref, grad_ref, act_ref, middle_ref, dh_ref, mine_ref, other_ref, rows_ref):
    conv_rows(middle_ref[...].astype(F32), dh_ref[...], FAR, rows_ref)
    for out_ref, core in ((mine_ref, core_ref[0]), (other_ref, 1 - core_ref[0])):
        acts = act_ref[pl.ds(pl.multiple_of(768 * core, 128), 768)]
        grad = mm(grad_ref[...], acts, 1, 1)
        for j in range(6):
            out_ref[CG * j : CG * (j + 1)] = grad[:, 128 * j : 128 * (j + 1)].astype(out_ref.dtype)
        out_ref[1152:] = rows_ref[pl.ds(pl.multiple_of(432 * core, 8), 432)].astype(out_ref.dtype)


def near_back_kernel(core_ref, got_ref, hidden_ref, start_ref, dh_ref, mine_ref, other_ref, rows_ref):
    da = sum(got_ref[j, :, :TOK].astype(F32) for j in range(8))
    hidden = hidden_ref[...]
    s = jax.nn.sigmoid(hidden)
    dh = (da * s * (1.0 + hidden * (1.0 - s))).astype(BF)
    dh_ref[...] = dh
    conv_rows(start_ref[...].astype(F32), dh, NEAR, rows_ref)
    for out_ref, core in ((mine_ref, core_ref[0]), (other_ref, 1 - core_ref[0])):
        out_ref[...] = rows_ref[pl.ds(pl.multiple_of(432 * core, 8), 432)].astype(out_ref.dtype)


def tokens_kernel(dh_ref, weight_ref, grad_ref, out_ref):
    back = grad_ref[...].astype(F32) + conv_back(dh_ref[...].astype(F32), weight_ref, NEAR)
    rows = back.T
    out_ref[:, :16] = rows[:, :128].reshape(32, 16, 128).astype(BF)
    rest = rows[:, 128:].reshape(32, 16, 64)
    out_ref[:, 16:] = jnp.concatenate([rest[:, :8], rest[:, 8:]], axis=2).astype(BF)


def gather_kernel(got_ref, early_ref, early_other_ref, late_ref, late_other_ref, tokens_ref, out_ref, rows_ref):
    rows_ref[:1584] = early_ref[...] + early_other_ref[...].astype(F32)
    rows_ref[1584:2016] = late_ref[...] + late_other_ref[...].astype(F32)
    rows_ref[2016:] = jnp.zeros((32, 128), F32)
    out_ref[:, :64] = rows_ref[...].reshape(32, 64, 128).astype(BF)
    out_ref[:, 64:ROWS] = got_ref[:, :160, TOK:].astype(F32).reshape(32, 40, 128).astype(BF)
    out_ref[:, ROWS:] = tokens_ref[...]


def sum_kernel(got_ref, out_ref):
    total = got_ref[0, :ROWS].astype(F32)
    for j in range(1, 32):
        total = total + got_ref[j, :ROWS].astype(F32)
    piece = (total * SCALE).astype(BF)
    for j in range(32):
        out_ref[j] = piece


def finish_kernel(core_ref, mine_ref, other_ref, near_pw_ref, far_pw_ref, near_conv_ref, far_conv_ref, all_ref, far_ref):
    first = core_ref[0] == 0
    mine = mine_ref[...].astype(F32)
    other = other_ref[...].astype(F32)
    all_ref[0] = jnp.where(first, mine, other)
    all_ref[1] = jnp.where(first, other, mine)
    for j in range(12):
        for part in range(3):
            near_pw_ref[64 * part : 64 * (part + 1), 128 * j : 128 * (j + 1)] = all_ref[
                j // 6, 3 * (j % 6) + part, :64
            ].astype(BF)
    for core in range(2):
        rows = all_ref[core, 18:, :64].reshape(14 * 64, 128)
        for out_ref, at in ((far_conv_ref, 0), (near_conv_ref, 432)):
            for block in range(9):
                place = 9 * core + block
                tap, column, half = place // 6, place // 2 % 3, place % 2
                out_ref[96 * tap + 48 * half : 96 * tap + 48 * (half + 1), 128 * column : 128 * (column + 1)] = rows[
                    at + 48 * block : at + 48 * (block + 1)
                ].astype(BF)
        for part in range(4):
            at = 96 * core + 24 * part
            for pair in range(4):
                blocks = []
                for j in (2 * pair, 2 * pair + 1):
                    piece = all_ref[core, 4 * j + part, 64:ROWS]
                    rest = jnp.concatenate([piece[24:32, :64], piece[24:32, 64:], piece[32:, :64]], axis=0)
                    blocks.append((piece[:24], rest))
                (even, even_rest), (odd, odd_rest) = blocks
                col = 2 * CG * pair
                far_ref[at : at + 24, col : col + 128] = even
                far_ref[at : at + 24, col + 128 : col + 256] = jnp.concatenate([even_rest, odd[:, :64]], axis=1)
                far_ref[at : at + 24, col + 256 : col + 384] = jnp.concatenate([odd[:, 64:], odd_rest], axis=1)
    far_pw_ref[...] = far_ref[...].astype(BF)


def slide(values, by):
    rows, cols = values.shape
    filler = jnp.zeros((rows, abs(by)), values.dtype)
    if by > 0:
        return jnp.concatenate([values[:, by:], filler], axis=1)
    return jnp.concatenate([filler, values[:, :by]], axis=1)


def local(emb, order, cot, cw1, pw1, cw2, pw2):
    core = lax.axis_index("core").astype(jnp.int32).reshape(1)
    base = (lax.axis_index(SEQ) * TOK).astype(jnp.int32).reshape(1)
    w1 = cw1.reshape(3, CG, CG)
    w2 = cw2.reshape(3, CG, CG)
    w1t = w1.transpose(0, 2, 1)
    pw1t = pw1.T
    pw2_blocks = pw2.reshape(CG, 8, CG).transpose(1, 0, 2)

    (packed,) = call(pack_kernel, [((TOK, 2 * CG), BF)], (base,), order.reshape(1, TOK), emb, cot)
    packed = swap(packed.reshape(32, TOK // 32, 2 * CG), CHIPS).reshape(TOK, 2 * CG)
    act8, near_hidden, start, cotq = call(
        near_kernel,
        [((8, CG, TOK), BF), ((CG, TOK), F32), ((CG, TOK), BF), ((CG, TOK), BF)],
        (),
        packed,
        w1t,
    )
    act_all = swap(act8, GRP).reshape(8 * CG, TOK)

    sent = jnp.concatenate([jnp.broadcast_to(cotq[None], (8, CG, TOK)), pw2_blocks], axis=2)
    sent = swap(sent, GRP)

    middle = (start.astype(F32) + mm(pw1, act_all, 1, 0)).astype(BF)
    far_hidden = (
        mm(w2[0], slide(middle, -FAR), 0, 0) + mm(w2[1], middle, 0, 0) + mm(w2[2], slide(middle, FAR), 0, 0)
    )
    far_act = jax.nn.silu(far_hidden).astype(BF)

    pg2_mine, pg2_other = call(
        regroup_kernel,
        [((8, 160, 128), F32), ((8, 160, 128), BF)],
        (core,),
        sent,
        far_act,
        scratch=[((8 * CG, CG), F32)],
    )
    pg2_other = other_core(pg2_other)
    far_dh, grad_middle = call(
        far_kernel, [((CG, TOK), BF), ((CG, TOK), BF)], (), sent, far_hidden, cotq, w2
    )
    (parts,) = call(parts_kernel, [((8, CG, TOK + 128), BF)], (), grad_middle, pw1t, pg2_mine, pg2_other)
    got = swap(parts, GRP)

    early, early_other = call(
        early_kernel,
        [((1584, 128), F32), ((1584, 128), BF)],
        (core,),
        grad_middle,
        act_all,
        middle,
        far_dh,
        scratch=[((864, 128), F32)],
    )
    early_other = other_core(early_other)

    near_dh, late, late_other = call(
        near_back_kernel,
        [((CG, TOK), BF), ((432, 128), F32), ((432, 128), BF)],
        (core,),
        got,
        near_hidden,
        start,
        scratch=[((864, 128), F32)],
    )
    late_other = other_core(late_other)
    (tokens,) = call(tokens_kernel, [((32, 24, 128), BF)], (), near_dh, w1, grad_middle)
    (bundle,) = call(
        gather_kernel,
        [((32, ROWS + 24, 128), BF)],
        (),
        got,
        early,
        early_other,
        late,
        late_other,
        tokens,
        scratch=[((2048, 128), F32)],
    )
    bundle = swap(bundle, CHIPS)
    (spread,) = call(sum_kernel, [((32, ROWS, 128), BF)], (), bundle)
    spread = swap(spread, CHIPS)

    rest = bundle[:, ROWS + 16 :]
    rest = jnp.concatenate([rest[:, :, :64], rest[:, :, 64:]], axis=1)
    back = jnp.concatenate([bundle[:, ROWS : ROWS + 16], rest], axis=2).reshape(TOK, CG)
    onehot = (lax.broadcasted_iota(jnp.int32, (TOK, TOK), 0) == (order - base)[None, :]).astype(BF)
    emb_grad = mm(back, onehot, 0, 1).astype(BF)

    out_pg1, out_pg2, out_cg1, out_cg2 = call(
        finish_kernel,
        [((CG, 8 * CG), BF), ((CG, 8 * CG), BF), ((288, 384), BF), ((288, 384), BF)],
        (core,),
        spread,
        other_core(spread),
        scratch=[((2, 32, ROWS, 128), F32), ((CG, 8 * CG), F32)],
    )
    flat = (1, 3 * CG * CG)
    return emb_grad, out_cg1.reshape(flat), out_pg1, out_cg2.reshape(flat), out_pg2


def solution(mesh):
    fine = Mesh(mesh.devices.reshape(4, 4, 2, 2, 4, 2), SEQ + GRP)
    placed = (P(GRP, SEQ), P(SEQ), P(GRP, SEQ), P(GRP, None), P(GRP, None), P(GRP, None), P(GRP, None))
    return jax.shard_map(
        local,
        mesh=fine,
        in_specs=placed,
        out_specs=(P(GRP, SEQ), P(GRP, None), P(GRP, None), P(GRP, None), P(GRP, None)),
        check_vma=False,
    )
```

```python
import jax
import jax.numpy as jnp
from jax import lax
from jax.experimental import pallas as pl
from jax.experimental.pallas import tpu as pltpu
from jax.sharding import Mesh, PartitionSpec as P

CG = 192
TOK = 512
NEAR = 32
FAR = 64
BF = jnp.bfloat16
F32 = jnp.float32
SEQ = ("zh", "yh", "yl", "core")
GRP = ("x", "zl")
CHIPS = ("zh", "yh", "yl")
SCALE = float(32768) ** (-0.5)
ROWS = 104


def mm(a, b, ca, cb):
    return lax.dot_general(a, b, (((ca,), (cb,)), ((), ())), preferred_element_type=F32)


def swap(blocks, axes):
    return lax.all_to_all(blocks, axes, 0, 0, tiled=True)


def other_core(values):
    return lax.ppermute(values, "core", [(0, 1), (1, 0)])


def call(kernel, outs, scalars, direct, fetched=(), scratch=(), mib=8, space=pl.ANY, flops=0):
    vmem = pl.BlockSpec(memory_space=pltpu.VMEM)
    smem = pl.BlockSpec(memory_space=pltpu.SMEM)
    anywhere = pl.BlockSpec(memory_space=space)
    n_near, n_far, n_out = len(scalars) + len(direct), len(fetched), len(outs)

    def body(*refs):
        near, far, out, rest = (
            refs[:n_near],
            refs[n_near : n_near + n_far],
            refs[n_near + n_far : n_near + n_far + n_out],
            refs[n_near + n_far + n_out :],
        )
        buffers, own = rest[:n_far], rest[n_far:]
        if n_far:
            sems, own = own[-1], own[:-1]
            copies = [pltpu.make_async_copy(far[i], buffers[i], sems.at[i]) for i in range(n_far)]
            for copy in copies:
                copy.start()
            for copy in copies:
                copy.wait()
        kernel(*near, *buffers, *out, *own)

    return pl.pallas_call(
        body,
        out_shape=[jax.ShapeDtypeStruct(shape, dtype) for shape, dtype in outs],
        in_specs=[smem] * len(scalars) + [vmem] * len(direct) + [anywhere] * n_far,
        out_specs=[vmem] * n_out,
        scratch_shapes=[pltpu.VMEM(x.shape, x.dtype) for x in fetched]
        + [pltpu.VMEM(shape, dtype) for shape, dtype in scratch]
        + ([pltpu.SemaphoreType.DMA((n_far,))] if n_far else []),
        compiler_params=pltpu.CompilerParams(vmem_limit_bytes=mib * 1024 * 1024),
        cost_estimate=pl.CostEstimate(flops=flops, bytes_accessed=0, transcendentals=0) if flops else None,
    )(*scalars, *direct, *fetched)


def shifted(values, by):
    if by == 0:
        return values.astype(BF)
    lane = lax.broadcasted_iota(jnp.int32, values.shape, 1)
    rolled = pltpu.roll(values, (-by) % TOK, 1)
    keep = lane < TOK - by if by > 0 else lane >= -by
    return jnp.where(keep, rolled, 0.0).astype(BF)


def conv_back(grads, weight_ref, by):
    return (
        mm(weight_ref[0], shifted(grads, by), 1, 0)
        + mm(weight_ref[1], shifted(grads, 0), 1, 0)
        + mm(weight_ref[2], shifted(grads, -by), 1, 0)
    )


def conv_rows(values, grads, by, rows_ref):
    row = lax.broadcasted_iota(jnp.int32, (CG, CG), 0)
    col = lax.broadcasted_iota(jnp.int32, (CG, CG), 1)
    half = CG // 2
    source = jnp.where(row < half, 2 * row, 2 * row - (CG - 1))
    order = jnp.where(col == source, 1.0, 0.0).astype(BF)
    for tap, distance in enumerate((-by, 0, by)):
        moved = mm(order, shifted(values, distance), 1, 0).astype(BF)
        grad = mm(moved, grads, 1, 1)
        even, odd = grad[:half], grad[half:]
        base = 3 * half * tap
        rows_ref[base : base + half] = even[:, :128]
        rows_ref[base + half : base + 2 * half] = jnp.concatenate([even[:, 128:], odd[:, :64]], axis=1)
        rows_ref[base + 2 * half : base + 3 * half] = odd[:, 64:]


def pack_kernel(base_ref, order_ref, emb_ref, cot_ref, out_ref):
    token = lax.broadcasted_iota(jnp.int32, (TOK, TOK), 0)
    onehot = jnp.where(token == order_ref[...] - base_ref[0], 1.0, 0.0).astype(BF)
    start = mm(emb_ref[...], onehot, 1, 0)
    both = jnp.concatenate([start, cot_ref[...].astype(F32)], axis=0)
    out_ref[...] = both.T.astype(BF)


def near_kernel(tokens_ref, weight_ref, blocks_ref, out_ref, hidden_ref, start_ref):
    rows = tokens_ref[...].astype(F32)
    both = rows.T
    start_ref[...] = both[:CG].astype(BF)
    cot = both[CG:].astype(BF)
    start = rows[:, :CG]
    filler = jnp.zeros((NEAR, CG), F32)
    before = jnp.concatenate([filler, start[: TOK - NEAR]], axis=0).astype(BF)
    after = jnp.concatenate([start[NEAR:], filler], axis=0).astype(BF)
    hidden = (
        mm(weight_ref[0], before, 0, 1)
        + mm(weight_ref[1], start.astype(BF), 0, 1)
        + mm(weight_ref[2], after, 0, 1)
    )
    hidden_ref[...] = hidden
    act = (hidden * jax.nn.sigmoid(hidden)).astype(BF)
    for j in range(8):
        out_ref[j, :, :TOK] = act
        out_ref[j, :, TOK : 2 * TOK] = cot
        out_ref[j, :, 2 * TOK :] = blocks_ref[j]


def mid_kernel(own_ref, sent_ref, start_ref, pointwise_ref, weight_ref, middle_ref, dh_ref, grad_ref, out_ref):
    middle = start_ref[...].astype(F32) + sum(
        mm(pointwise_ref[j * CG : (j + 1) * CG], sent_ref[j, :, :TOK], 0, 0) for j in range(8)
    )
    middle = middle.astype(BF)
    middle_ref[...] = middle
    wide = middle.astype(F32)
    hidden = (
        mm(weight_ref[0], shifted(wide, -FAR), 0, 0)
        + mm(weight_ref[1], middle, 0, 0)
        + mm(weight_ref[2], shifted(wide, FAR), 0, 0)
    )
    s = jax.nn.sigmoid(hidden)
    act = (hidden * s).astype(BF)
    for j in range(8):
        out_ref[j, :, TOK:] = mm(sent_ref[j, :, TOK : 2 * TOK], act, 1, 1).astype(BF)
    da = sum(mm(sent_ref[j, :, 2 * TOK :], sent_ref[j, :, TOK : 2 * TOK], 0, 0) for j in range(8))
    dh = (da * s * (1.0 + hidden * (1.0 - s))).astype(BF)
    dh_ref[...] = dh
    back = conv_back(dh.astype(F32), weight_ref, FAR)
    grad = (sent_ref[own_ref[0], :, TOK : 2 * TOK].astype(F32) + back).astype(BF)
    grad_ref[...] = grad
    for j in range(8):
        out_ref[j, :, :TOK] = mm(pointwise_ref[j * CG : (j + 1) * CG], grad, 1, 0).astype(BF)


def back_kernel(
    core_ref,
    got_ref,
    sent_ref,
    hidden_ref,
    start_ref,
    grad_ref,
    middle_ref,
    far_dh_ref,
    dh_ref,
    mine_ref,
    other_ref,
    far_rows_ref,
    near_rows_ref,
):
    da = sum(got_ref[j, :, :TOK].astype(F32) for j in range(8))
    hidden = hidden_ref[...]
    s = jax.nn.sigmoid(hidden)
    dh = (da * s * (1.0 + hidden * (1.0 - s))).astype(BF)
    dh_ref[...] = dh
    conv_rows(start_ref[...].astype(F32), dh, NEAR, near_rows_ref)
    conv_rows(middle_ref[...].astype(F32), far_dh_ref[...], FAR, far_rows_ref)
    blank = jnp.zeros((8, 64), F32)
    for out_ref, core in ((mine_ref, core_ref[0]), (other_ref, 1 - core_ref[0])):
        grad = jnp.concatenate([mm(grad_ref[...], sent_ref[4 * core + j, :, :TOK], 1, 1) for j in range(4)], axis=1)
        for j in range(6):
            out_ref[CG * j : CG * (j + 1)] = grad[:, 128 * j : 128 * (j + 1)].astype(out_ref.dtype)
        rows = pl.ds(pl.multiple_of(432 * core, 8), 432)
        out_ref[1152:1584] = far_rows_ref[rows].astype(out_ref.dtype)
        out_ref[1584:2016] = near_rows_ref[rows].astype(out_ref.dtype)
        for j in range(8):
            half = got_ref[j, pl.ds(pl.multiple_of(96 * core, 16), 96), TOK:].astype(F32)
            for part in range(4):
                piece = half[24 * part : 24 * (part + 1)]
                rest = piece[:, 128:]
                packed = jnp.concatenate([rest[:8], rest[8:16]], axis=1), jnp.concatenate([rest[16:], blank], axis=1)
                at = 2016 + 160 * j + 40 * part
                out_ref[at : at + 40] = jnp.concatenate([piece[:, :128], *packed], axis=0).astype(out_ref.dtype)


def tokens_kernel(dh_ref, weight_ref, grad_ref, out_ref):
    back = grad_ref[...].astype(F32) + conv_back(dh_ref[...].astype(F32), weight_ref, NEAR)
    rows = back.T
    out_ref[:, :16] = rows[:, :128].reshape(32, 16, 128).astype(BF)
    rest = rows[:, 128:].reshape(32, 16, 64)
    out_ref[:, 16:] = jnp.concatenate([rest[:, :8], rest[:, 8:]], axis=2).astype(BF)


def gather_kernel(mine_ref, other_ref, tokens_ref, out_ref, rows_ref):
    rows_ref[:2016] = mine_ref[:2016] + other_ref[:2016].astype(F32)
    rows_ref[2016:] = jnp.zeros((32, 128), F32)
    out_ref[:, :64] = rows_ref[...].reshape(32, 64, 128).astype(BF)
    rest = mine_ref[2016:] + other_ref[2016:].astype(F32)
    out_ref[:, 64:ROWS] = rest.reshape(32, 40, 128).astype(BF)
    out_ref[:, ROWS:] = tokens_ref[...]


def sum_kernel(got_ref, out_ref):
    total = got_ref[0, :ROWS].astype(F32)
    for j in range(1, 32):
        total = total + got_ref[j, :ROWS].astype(F32)
    piece = (total * SCALE).astype(BF)
    for j in range(32):
        out_ref[j] = piece


def finish_kernel(core_ref, mine_ref, other_ref, near_pw_ref, far_pw_ref, near_conv_ref, far_conv_ref, all_ref, far_ref):
    first = core_ref[0] == 0
    mine = mine_ref[...].astype(F32)
    other = other_ref[...].astype(F32)
    all_ref[0] = jnp.where(first, mine, other)
    all_ref[1] = jnp.where(first, other, mine)
    for j in range(12):
        for part in range(3):
            near_pw_ref[64 * part : 64 * (part + 1), 128 * j : 128 * (j + 1)] = all_ref[
                j // 6, 3 * (j % 6) + part, :64
            ].astype(BF)
    for core in range(2):
        rows = all_ref[core, 18:, :64].reshape(14 * 64, 128)
        for out_ref, at in ((far_conv_ref, 0), (near_conv_ref, 432)):
            for block in range(9):
                place = 9 * core + block
                tap, column, half = place // 6, place // 2 % 3, place % 2
                out_ref[96 * tap + 48 * half : 96 * tap + 48 * (half + 1), 128 * column : 128 * (column + 1)] = rows[
                    at + 48 * block : at + 48 * (block + 1)
                ].astype(BF)
        for part in range(4):
            at = 96 * core + 24 * part
            for pair in range(4):
                blocks = []
                for j in (2 * pair, 2 * pair + 1):
                    piece = all_ref[core, 4 * j + part, 64:ROWS]
                    rest = jnp.concatenate([piece[24:32, :64], piece[24:32, 64:], piece[32:, :64]], axis=0)
                    blocks.append((piece[:24], rest))
                (even, even_rest), (odd, odd_rest) = blocks
                col = 2 * CG * pair
                far_ref[at : at + 24, col : col + 128] = even
                far_ref[at : at + 24, col + 128 : col + 256] = jnp.concatenate([even_rest, odd[:, :64]], axis=1)
                far_ref[at : at + 24, col + 256 : col + 384] = jnp.concatenate([odd[:, 64:], odd_rest], axis=1)
    far_pw_ref[...] = far_ref[...].astype(BF)


def local(emb, order, cot, cw1, pw1, cw2, pw2):
    core = lax.axis_index("core").astype(jnp.int32).reshape(1)
    own = lax.axis_index(GRP).astype(jnp.int32).reshape(1)
    base = (lax.axis_index(SEQ) * TOK).astype(jnp.int32).reshape(1)

    (packed,) = call(pack_kernel, [((TOK, 2 * CG), BF)], (base,), (), (order.reshape(1, TOK), emb, cot), space=pltpu.HBM)
    packed = swap(packed.reshape(32, TOK // 32, 2 * CG), CHIPS).reshape(TOK, 2 * CG)
    packed, own, core, w1, w2, pw1t, pw2_blocks = lax.optimization_barrier(
        (packed, own, core, cw1.reshape(3, CG, CG), cw2.reshape(3, CG, CG), pw1.T, pw2.reshape(CG, 8, CG).transpose(1, 0, 2))
    )
    sent, near_hidden, start = call(
        near_kernel,
        [((8, CG, 2 * TOK + CG), BF), ((CG, TOK), F32), ((CG, TOK), BF)],
        (),
        (packed, w1, pw2_blocks),
    )
    sent = swap(sent, GRP)
    middle, far_dh, grad_middle, parts = call(
        mid_kernel,
        [((CG, TOK), BF), ((CG, TOK), BF), ((CG, TOK), BF), ((8, CG, TOK + CG), BF)],
        (own,),
        (sent,),
        (start, pw1t, w2),
    )
    got = swap(parts, GRP)

    near_dh, mine, other = call(
        back_kernel,
        [((CG, TOK), BF), ((3296, 128), F32), ((3296, 128), BF)],
        (core,),
        (got, sent),
        (near_hidden, start, grad_middle, middle, far_dh),
        scratch=[((864, 128), F32), ((864, 128), F32)],
    )
    other = other_core(other)
    (tokens,) = call(tokens_kernel, [((32, 24, 128), BF)], (), (near_dh,), (w1, grad_middle))
    (bundle,) = call(
        gather_kernel,
        [((32, ROWS + 24, 128), BF)],
        (),
        (),
        (mine, other, tokens),
        scratch=[((2048, 128), F32)],
    )
    bundle = swap(bundle, CHIPS)
    (spread,) = call(sum_kernel, [((32, ROWS, 128), BF)], (), (bundle,))
    spread = swap(spread, CHIPS)

    rest = bundle[:, ROWS + 16 :]
    rest = jnp.concatenate([rest[:, :, :64], rest[:, :, 64:]], axis=1)
    back = jnp.concatenate([bundle[:, ROWS : ROWS + 16], rest], axis=2).reshape(TOK, CG)
    onehot = (lax.broadcasted_iota(jnp.int32, (TOK, TOK), 0) == (order - base)[None, :]).astype(BF)
    emb_grad = mm(back, onehot, 0, 1).astype(BF)

    out_pg1, out_pg2, out_cg1, out_cg2 = call(
        finish_kernel,
        [((CG, 8 * CG), BF), ((CG, 8 * CG), BF), ((288, 384), BF), ((288, 384), BF)],
        (core,),
        (spread, other_core(spread)),
        scratch=[((2, 32, ROWS, 128), F32), ((CG, 8 * CG), F32)],
        mib=12,
    )
    flat = (1, 3 * CG * CG)
    return emb_grad, out_cg1.reshape(flat), out_pg1, out_cg2.reshape(flat), out_pg2


def solution(mesh):
    fine = Mesh(mesh.devices.reshape(4, 4, 2, 2, 4, 2), SEQ + GRP)
    placed = (P(GRP, SEQ), P(SEQ), P(GRP, SEQ), P(GRP, None), P(GRP, None), P(GRP, None), P(GRP, None))
    return jax.shard_map(
        local,
        mesh=fine,
        in_specs=placed,
        out_specs=(P(GRP, SEQ), P(GRP, None), P(GRP, None), P(GRP, None), P(GRP, None)),
        check_vma=False,
    )
```

```python
import jax
import jax.numpy as jnp
from jax import lax
from jax.experimental import pallas as pl
from jax.experimental.pallas import tpu as pltpu
from jax.sharding import Mesh, PartitionSpec as P

CG = 192
TOK = 512
NEAR = 32
FAR = 64
BF = jnp.bfloat16
F32 = jnp.float32
SEQ = ("zh", "yh", "yl", "core")
GRP = ("x", "zl")
CHIPS = ("zh", "yh", "yl")
SCALE = float(32768) ** (-0.5)
ROWS = 104


def mm(a, b, ca, cb):
    return lax.dot_general(a, b, (((ca,), (cb,)), ((), ())), preferred_element_type=F32)


def swap(blocks, axes):
    return lax.all_to_all(blocks, axes, 0, 0, tiled=True)


def other_core(values):
    return lax.ppermute(values, "core", [(0, 1), (1, 0)])


def call(kernel, outs, scalars, direct, fetched=(), scratch=(), mib=8, space=pl.ANY, flops=0):
    vmem = pl.BlockSpec(memory_space=pltpu.VMEM)
    smem = pl.BlockSpec(memory_space=pltpu.SMEM)
    anywhere = pl.BlockSpec(memory_space=space)
    n_near, n_far, n_out = len(scalars) + len(direct), len(fetched), len(outs)

    def body(*refs):
        near, far, out, rest = (
            refs[:n_near],
            refs[n_near : n_near + n_far],
            refs[n_near + n_far : n_near + n_far + n_out],
            refs[n_near + n_far + n_out :],
        )
        buffers, own = rest[:n_far], rest[n_far:]
        if n_far:
            sems, own = own[-1], own[:-1]
            copies = [pltpu.make_async_copy(far[i], buffers[i], sems.at[i]) for i in range(n_far)]
            for copy in copies:
                copy.start()
            for copy in copies:
                copy.wait()
        kernel(*near, *buffers, *out, *own)

    return pl.pallas_call(
        body,
        out_shape=[jax.ShapeDtypeStruct(shape, dtype) for shape, dtype in outs],
        in_specs=[smem] * len(scalars) + [vmem] * len(direct) + [anywhere] * n_far,
        out_specs=[vmem] * n_out,
        scratch_shapes=[pltpu.VMEM(x.shape, x.dtype) for x in fetched]
        + [pltpu.VMEM(shape, dtype) for shape, dtype in scratch]
        + ([pltpu.SemaphoreType.DMA((n_far,))] if n_far else []),
        compiler_params=pltpu.CompilerParams(vmem_limit_bytes=mib * 1024 * 1024),
        cost_estimate=pl.CostEstimate(flops=flops, bytes_accessed=0, transcendentals=0) if flops else None,
    )(*scalars, *direct, *fetched)


def shifted(values, by):
    if by == 0:
        return values.astype(BF)
    lane = lax.broadcasted_iota(jnp.int32, values.shape, 1)
    rolled = pltpu.roll(values, (-by) % TOK, 1)
    keep = lane < TOK - by if by > 0 else lane >= -by
    return jnp.where(keep, rolled, 0.0).astype(BF)


def conv_back(grads, weight_ref, by):
    return (
        mm(weight_ref[0], shifted(grads, by), 1, 0)
        + mm(weight_ref[1], shifted(grads, 0), 1, 0)
        + mm(weight_ref[2], shifted(grads, -by), 1, 0)
    )


def conv_rows(values, grads, by, rows_ref):
    row = lax.broadcasted_iota(jnp.int32, (CG, CG), 0)
    col = lax.broadcasted_iota(jnp.int32, (CG, CG), 1)
    half = CG // 2
    source = jnp.where(row < half, 2 * row, 2 * row - (CG - 1))
    order = jnp.where(col == source, 1.0, 0.0).astype(BF)
    for tap, distance in enumerate((-by, 0, by)):
        moved = mm(order, shifted(values, distance), 1, 0).astype(BF)
        grad = mm(moved, grads, 1, 1)
        even, odd = grad[:half], grad[half:]
        base = 3 * half * tap
        rows_ref[base : base + half] = even[:, :128]
        rows_ref[base + half : base + 2 * half] = jnp.concatenate([even[:, 128:], odd[:, :64]], axis=1)
        rows_ref[base + 2 * half : base + 3 * half] = odd[:, 64:]


def pack_kernel(base_ref, order_ref, emb_ref, cot_ref, out_ref):
    token = lax.broadcasted_iota(jnp.int32, (TOK, TOK), 0)
    onehot = jnp.where(token == order_ref[...] - base_ref[0], 1.0, 0.0).astype(BF)
    start = mm(emb_ref[...], onehot, 1, 0)
    both = jnp.concatenate([start, cot_ref[...].astype(F32)], axis=0)
    out_ref[...] = both.T.astype(BF)


def pieces_kernel(own_ref, weight_ref, *refs):
    outs, slots_ref = refs[:8], refs[8]
    own = own_ref[0]
    for j in range(8):
        step = (j // 2 + 4 - own // 2) % 4
        flip = (j % 2 + own) % 2
        slots_ref[2 * step + flip] = weight_ref[:, j * CG : (j + 1) * CG]
    for j in range(8):
        outs[j][...] = slots_ref[j]


def near_kernel(tokens_ref, weight_ref, out_ref, hidden_ref, start_ref):
    rows = tokens_ref[...].astype(F32)
    both = rows.T
    start_ref[...] = both[:CG].astype(BF)
    cot = both[CG:].astype(BF)
    start = rows[:, :CG]
    filler = jnp.zeros((NEAR, CG), F32)
    before = jnp.concatenate([filler, start[: TOK - NEAR]], axis=0).astype(BF)
    after = jnp.concatenate([start[NEAR:], filler], axis=0).astype(BF)
    hidden = (
        mm(weight_ref[0], before, 0, 1)
        + mm(weight_ref[1], start.astype(BF), 0, 1)
        + mm(weight_ref[2], after, 0, 1)
    )
    hidden_ref[...] = hidden
    act = (hidden * jax.nn.sigmoid(hidden)).astype(BF)
    for j in range(8):
        out_ref[j, :, :TOK] = act
        out_ref[j, :, TOK:] = cot


def mid_kernel(own_ref, sent_ref, start_ref, pointwise_ref, weight_ref, *refs):
    columns, (middle_ref, dh_ref, grad_ref, out_ref) = refs[:8], refs[8:]
    middle = start_ref[...].astype(F32) + sum(
        mm(pointwise_ref[j * CG : (j + 1) * CG], sent_ref[j, :, :TOK], 0, 0) for j in range(8)
    )
    middle = middle.astype(BF)
    middle_ref[...] = middle
    wide = middle.astype(F32)
    hidden = (
        mm(weight_ref[0], shifted(wide, -FAR), 0, 0)
        + mm(weight_ref[1], middle, 0, 0)
        + mm(weight_ref[2], shifted(wide, FAR), 0, 0)
    )
    s = jax.nn.sigmoid(hidden)
    act = (hidden * s).astype(BF)
    for j in range(8):
        grad = mm(sent_ref[j, :, TOK:], act, 1, 1)
        rest = grad[:, 128:]
        rows = jnp.concatenate([grad[:, :128], jnp.concatenate([rest[:96], rest[96:]], axis=1)], axis=0)
        for part in range(4):
            out_ref[j, CG:, 128 * part : 128 * (part + 1)] = rows[72 * part : 72 * (part + 1)].astype(BF)
    own = own_ref[0]
    da = jnp.zeros((CG, TOK), F32)
    for j in range(8):
        source = 2 * ((own // 2 + 4 - j // 2) % 4) + (own + j) % 2
        da = da + mm(columns[j][...], sent_ref[source, :, TOK:], 0, 0)
    dh = (da * s * (1.0 + hidden * (1.0 - s))).astype(BF)
    dh_ref[...] = dh
    back = conv_back(dh.astype(F32), weight_ref, FAR)
    grad = (sent_ref[own, :, TOK:].astype(F32) + back).astype(BF)
    grad_ref[...] = grad
    for j in range(8):
        out_ref[j, :CG] = mm(pointwise_ref[j * CG : (j + 1) * CG], grad, 1, 0).astype(BF)


def back_kernel(
    core_ref,
    got_ref,
    sent_ref,
    hidden_ref,
    start_ref,
    grad_ref,
    middle_ref,
    far_dh_ref,
    dh_ref,
    mine_ref,
    other_ref,
    far_rows_ref,
    near_rows_ref,
    seq_ref,
):
    for j in range(8):
        for part in range(4):
            seq_ref[j, 72 * part : 72 * (part + 1)] = got_ref[j, CG:, 128 * part : 128 * (part + 1)].astype(F32)
    da = sum(got_ref[j, :CG].astype(F32) for j in range(8))
    hidden = hidden_ref[...]
    s = jax.nn.sigmoid(hidden)
    dh = (da * s * (1.0 + hidden * (1.0 - s))).astype(BF)
    dh_ref[...] = dh
    conv_rows(start_ref[...].astype(F32), dh, NEAR, near_rows_ref)
    conv_rows(middle_ref[...].astype(F32), far_dh_ref[...], FAR, far_rows_ref)
    blank = jnp.zeros((8, 64), F32)
    for out_ref, core in ((mine_ref, core_ref[0]), (other_ref, 1 - core_ref[0])):
        grad = jnp.concatenate([mm(grad_ref[...], sent_ref[4 * core + j, :, :TOK], 1, 1) for j in range(4)], axis=1)
        for j in range(6):
            out_ref[CG * j : CG * (j + 1)] = grad[:, 128 * j : 128 * (j + 1)].astype(out_ref.dtype)
        rows = pl.ds(pl.multiple_of(432 * core, 8), 432)
        out_ref[1152:1584] = far_rows_ref[rows].astype(out_ref.dtype)
        out_ref[1584:2016] = near_rows_ref[rows].astype(out_ref.dtype)
        for j in range(8):
            wide = seq_ref[j, pl.ds(pl.multiple_of(96 * core, 8), 96)]
            thin = jnp.where(core == 0, seq_ref[j, CG:, :64], seq_ref[j, CG:, 64:])
            for part in range(4):
                piece = wide[24 * part : 24 * (part + 1)]
                rest = thin[24 * part : 24 * (part + 1)]
                packed = jnp.concatenate([rest[:8], rest[8:16]], axis=1), jnp.concatenate([rest[16:], blank], axis=1)
                at = 2016 + 160 * j + 40 * part
                out_ref[at : at + 40] = jnp.concatenate([piece, *packed], axis=0).astype(out_ref.dtype)


def tokens_kernel(dh_ref, weight_ref, grad_ref, out_ref):
    back = grad_ref[...].astype(F32) + conv_back(dh_ref[...].astype(F32), weight_ref, NEAR)
    rows = back.T
    out_ref[:, :16] = rows[:, :128].reshape(32, 16, 128).astype(BF)
    rest = rows[:, 128:].reshape(32, 16, 64)
    out_ref[:, 16:] = jnp.concatenate([rest[:, :8], rest[:, 8:]], axis=2).astype(BF)


def gather_kernel(mine_ref, other_ref, tokens_ref, out_ref, rows_ref):
    rows_ref[:2016] = mine_ref[:2016] + other_ref[:2016].astype(F32)
    rows_ref[2016:] = jnp.zeros((32, 128), F32)
    out_ref[:, :64] = rows_ref[...].reshape(32, 64, 128).astype(BF)
    rest = mine_ref[2016:] + other_ref[2016:].astype(F32)
    out_ref[:, 64:ROWS] = rest.reshape(32, 40, 128).astype(BF)
    out_ref[:, ROWS:] = tokens_ref[...]


def sum_kernel(got_ref, out_ref):
    total = got_ref[0, :ROWS].astype(F32)
    for j in range(1, 32):
        total = total + got_ref[j, :ROWS].astype(F32)
    piece = (total * SCALE).astype(BF)
    for j in range(32):
        out_ref[j] = piece


def finish_kernel(core_ref, mine_ref, other_ref, near_pw_ref, far_pw_ref, near_conv_ref, far_conv_ref, all_ref, far_ref):
    first = core_ref[0] == 0
    mine = mine_ref[...].astype(F32)
    other = other_ref[...].astype(F32)
    all_ref[0] = jnp.where(first, mine, other)
    all_ref[1] = jnp.where(first, other, mine)
    for j in range(12):
        for part in range(3):
            near_pw_ref[64 * part : 64 * (part + 1), 128 * j : 128 * (j + 1)] = all_ref[
                j // 6, 3 * (j % 6) + part, :64
            ].astype(BF)
    for core in range(2):
        rows = all_ref[core, 18:, :64].reshape(14 * 64, 128)
        for out_ref, at in ((far_conv_ref, 0), (near_conv_ref, 432)):
            for block in range(9):
                place = 9 * core + block
                tap, column, half = place // 6, place // 2 % 3, place % 2
                out_ref[96 * tap + 48 * half : 96 * tap + 48 * (half + 1), 128 * column : 128 * (column + 1)] = rows[
                    at + 48 * block : at + 48 * (block + 1)
                ].astype(BF)
        for part in range(4):
            at = 96 * core + 24 * part
            for pair in range(4):
                blocks = []
                for j in (2 * pair, 2 * pair + 1):
                    piece = all_ref[core, 4 * j + part, 64:ROWS]
                    rest = jnp.concatenate([piece[24:32, :64], piece[24:32, 64:], piece[32:, :64]], axis=0)
                    blocks.append((piece[:24], rest))
                (even, even_rest), (odd, odd_rest) = blocks
                col = 2 * CG * pair
                far_ref[at : at + 24, col : col + 128] = even
                far_ref[at : at + 24, col + 128 : col + 256] = jnp.concatenate([even_rest, odd[:, :64]], axis=1)
                far_ref[at : at + 24, col + 256 : col + 384] = jnp.concatenate([odd[:, 64:], odd_rest], axis=1)
    far_pw_ref[...] = far_ref[...].astype(BF)


def step(emb, order, cot, cw1, pw1, cw2, pw2):
    core = lax.axis_index("core").astype(jnp.int32).reshape(1)
    own = lax.axis_index(GRP).astype(jnp.int32).reshape(1)
    base = (lax.axis_index(SEQ) * TOK).astype(jnp.int32).reshape(1)

    (packed,) = call(pack_kernel, [((TOK, 2 * CG), BF)], (base,), (), (order.reshape(1, TOK), emb, cot), space=pltpu.HBM)
    packed = swap(packed.reshape(32, TOK // 32, 2 * CG), CHIPS).reshape(TOK, 2 * CG)
    pieces = call(pieces_kernel, [((CG, CG), BF)] * 8, (own,), (), (pw2,), scratch=[((8, CG, CG), BF)])
    columns = [pieces[0]]
    for j in range(1, 8):
        route = [(a, 2 * ((a // 2 + j // 2) % 4) + (a + j) % 2) for a in range(8)]
        columns.append(lax.ppermute(pieces[j], GRP, route))
    packed, own, core, w1, w2, pw1t, columns = lax.optimization_barrier(
        (packed, own, core, cw1.reshape(3, CG, CG), cw2.reshape(3, CG, CG), pw1.T, columns)
    )
    sent, near_hidden, start = call(
        near_kernel,
        [((8, CG, 2 * TOK), BF), ((CG, TOK), F32), ((CG, TOK), BF)],
        (),
        (packed, w1),
    )
    sent = swap(sent, GRP)
    middle, far_dh, grad_middle, parts = call(
        mid_kernel,
        [((CG, TOK), BF), ((CG, TOK), BF), ((CG, TOK), BF), ((8, CG + 72, TOK), BF)],
        (own,),
        (sent,),
        (start, pw1t, w2, *columns),
    )
    got = swap(parts, GRP)

    near_dh, mine, other = call(
        back_kernel,
        [((CG, TOK), BF), ((3296, 128), F32), ((3296, 128), BF)],
        (core,),
        (got, sent),
        (near_hidden, start, grad_middle, middle, far_dh),
        scratch=[((864, 128), F32), ((864, 128), F32), ((8, 288, 128), F32)],
    )
    other = other_core(other)
    (tokens,) = call(tokens_kernel, [((32, 24, 128), BF)], (), (near_dh,), (w1, grad_middle))
    (bundle,) = call(
        gather_kernel,
        [((32, ROWS + 24, 128), BF)],
        (),
        (),
        (mine, other, tokens),
        scratch=[((2048, 128), F32)],
    )
    bundle = swap(bundle, CHIPS)
    (spread,) = call(sum_kernel, [((32, ROWS, 128), BF)], (), (bundle,))
    spread = swap(spread, CHIPS)

    rest = bundle[:, ROWS + 16 :]
    rest = jnp.concatenate([rest[:, :, :64], rest[:, :, 64:]], axis=1)
    back = jnp.concatenate([bundle[:, ROWS : ROWS + 16], rest], axis=2).reshape(TOK, CG)
    onehot = (lax.broadcasted_iota(jnp.int32, (TOK, TOK), 0) == (order - base)[None, :]).astype(BF)
    emb_grad = mm(back, onehot, 0, 1).astype(BF)

    out_pg1, out_pg2, out_cg1, out_cg2 = call(
        finish_kernel,
        [((CG, 8 * CG), BF), ((CG, 8 * CG), BF), ((288, 384), BF), ((288, 384), BF)],
        (core,),
        (spread, other_core(spread)),
        scratch=[((2, 32, ROWS, 128), F32), ((CG, 8 * CG), F32)],
        mib=12,
    )
    flat = (1, 3 * CG * CG)
    return emb_grad, out_cg1.reshape(flat), out_pg1, out_cg2.reshape(flat), out_pg2


def solution(mesh):
    fine = Mesh(mesh.devices.reshape(4, 4, 2, 2, 4, 2), SEQ + GRP)
    placed = (P(GRP, SEQ), P(SEQ), P(GRP, SEQ), P(GRP, None), P(GRP, None), P(GRP, None), P(GRP, None))
    return jax.shard_map(
        step,
        mesh=fine,
        in_specs=placed,
        out_specs=(P(GRP, SEQ), P(GRP, None), P(GRP, None), P(GRP, None), P(GRP, None)),
        check_vma=False,
    )
```

```python
import jax
import jax.numpy as jnp
from jax import lax
from jax.experimental import pallas as pl
from jax.experimental.pallas import tpu as pltpu
from jax.sharding import Mesh, PartitionSpec as P

CG = 192
TOK = 512
NEAR = 32
FAR = 64
BF = jnp.bfloat16
F32 = jnp.float32
SEQ = ("zh", "yh", "yl", "core")
GRP = ("x", "zl")
CHIPS = ("zh", "yh", "yl")
SCALE = float(32768) ** (-0.5)
ROWS = 104


def mm(a, b, ca, cb):
    return lax.dot_general(a, b, (((ca,), (cb,)), ((), ())), preferred_element_type=F32)


def swap(blocks, axes):
    return lax.all_to_all(blocks, axes, 0, 0, tiled=True)


def other_core(values):
    return lax.ppermute(values, "core", [(0, 1), (1, 0)])


def call(kernel, outs, scalars, direct, fetched=(), scratch=(), mib=8, space=pl.ANY, flops=0):
    vmem = pl.BlockSpec(memory_space=pltpu.VMEM)
    smem = pl.BlockSpec(memory_space=pltpu.SMEM)
    anywhere = pl.BlockSpec(memory_space=space)
    n_near, n_far, n_out = len(scalars) + len(direct), len(fetched), len(outs)

    def body(*refs):
        near, far, out, rest = (
            refs[:n_near],
            refs[n_near : n_near + n_far],
            refs[n_near + n_far : n_near + n_far + n_out],
            refs[n_near + n_far + n_out :],
        )
        buffers, own = rest[:n_far], rest[n_far:]
        if n_far:
            sems, own = own[-1], own[:-1]
            copies = [pltpu.make_async_copy(far[i], buffers[i], sems.at[i]) for i in range(n_far)]
            for copy in copies:
                copy.start()
            for copy in copies:
                copy.wait()
        kernel(*near, *buffers, *out, *own)

    return pl.pallas_call(
        body,
        out_shape=[jax.ShapeDtypeStruct(shape, dtype) for shape, dtype in outs],
        in_specs=[smem] * len(scalars) + [vmem] * len(direct) + [anywhere] * n_far,
        out_specs=[vmem] * n_out,
        scratch_shapes=[pltpu.VMEM(x.shape, x.dtype) for x in fetched]
        + [pltpu.VMEM(shape, dtype) for shape, dtype in scratch]
        + ([pltpu.SemaphoreType.DMA((n_far,))] if n_far else []),
        compiler_params=pltpu.CompilerParams(vmem_limit_bytes=mib * 1024 * 1024),
        cost_estimate=pl.CostEstimate(flops=flops, bytes_accessed=0, transcendentals=0) if flops else None,
    )(*scalars, *direct, *fetched)


def shifted(values, by):
    if by == 0:
        return values.astype(BF)
    lane = lax.broadcasted_iota(jnp.int32, values.shape, 1)
    rolled = pltpu.roll(values, (-by) % TOK, 1)
    keep = lane < TOK - by if by > 0 else lane >= -by
    return jnp.where(keep, rolled, 0.0).astype(BF)


def conv_back(grads, weight_ref, by):
    return (
        mm(weight_ref[0], shifted(grads, by), 1, 0)
        + mm(weight_ref[1], shifted(grads, 0), 1, 0)
        + mm(weight_ref[2], shifted(grads, -by), 1, 0)
    )


def conv_rows(values, grads, by, rows_ref):
    row = lax.broadcasted_iota(jnp.int32, (CG, CG), 0)
    col = lax.broadcasted_iota(jnp.int32, (CG, CG), 1)
    half = CG // 2
    source = jnp.where(row < half, 2 * row, 2 * row - (CG - 1))
    order = jnp.where(col == source, 1.0, 0.0).astype(BF)
    for tap, distance in enumerate((-by, 0, by)):
        moved = mm(order, shifted(values, distance), 1, 0).astype(BF)
        grad = mm(moved, grads, 1, 1)
        even, odd = grad[:half], grad[half:]
        base = 3 * half * tap
        rows_ref[base : base + half] = even[:, :128]
        rows_ref[base + half : base + 2 * half] = jnp.concatenate([even[:, 128:], odd[:, :64]], axis=1)
        rows_ref[base + 2 * half : base + 3 * half] = odd[:, 64:]


def pack_kernel(base_ref, both_ref, order_ref, out_ref):
    token = lax.broadcasted_iota(jnp.int32, (TOK, TOK), 0)
    onehot = jnp.where(token == order_ref[...] - base_ref[0], 1.0, 0.0).astype(BF)
    start = mm(both_ref[:CG], onehot, 1, 0)
    both = jnp.concatenate([start, both_ref[CG:].astype(F32)], axis=0)
    out_ref[...] = both.T.astype(BF)


def halves_kernel(core_ref, weight_ref, out_ref):
    half = weight_ref[pl.ds(pl.multiple_of(96 * core_ref[0], 16), 96)].astype(F32)
    blank = jnp.zeros((96, 64), F32)
    for j in range(8):
        block = half[:, CG * j : CG * (j + 1)]
        out_ref[j, :96] = block[:, :128].astype(BF)
        out_ref[j, 96:] = jnp.concatenate([block[:, 128:], blank], axis=1).astype(BF)


def near_kernel(tokens_ref, weight_ref, blocks_ref, out_ref, hidden_ref, start_ref):
    rows = tokens_ref[...].astype(F32)
    both = rows.T
    start_ref[...] = both[:CG].astype(BF)
    cot = both[CG:].astype(BF)
    start = rows[:, :CG]
    filler = jnp.zeros((NEAR, CG), F32)
    before = jnp.concatenate([filler, start[: TOK - NEAR]], axis=0).astype(BF)
    after = jnp.concatenate([start[NEAR:], filler], axis=0).astype(BF)
    hidden = (
        mm(weight_ref[0], before, 0, 1)
        + mm(weight_ref[1], start.astype(BF), 0, 1)
        + mm(weight_ref[2], after, 0, 1)
    )
    hidden_ref[...] = hidden
    act = (hidden * jax.nn.sigmoid(hidden)).astype(BF)
    for j in range(8):
        out_ref[j, :, :TOK] = act
        out_ref[j, :, TOK : 2 * TOK] = cot
        out_ref[j, :, 2 * TOK :] = blocks_ref[j]


def mid_kernel(sent_ref, start_ref, pointwise_ref, weight_ref, middle_ref, hidden_ref, rows_ref):
    middle = start_ref[...].astype(F32) + sum(
        mm(pointwise_ref[j * CG : (j + 1) * CG], sent_ref[j, :, :TOK], 0, 0) for j in range(8)
    )
    middle = middle.astype(BF)
    middle_ref[...] = middle
    wide = middle.astype(F32)
    hidden = (
        mm(weight_ref[0], shifted(wide, -FAR), 0, 0)
        + mm(weight_ref[1], middle, 0, 0)
        + mm(weight_ref[2], shifted(wide, FAR), 0, 0)
    )
    hidden_ref[...] = hidden
    act = (hidden * jax.nn.sigmoid(hidden)).astype(BF)
    blank = jnp.zeros((64, TOK), BF)
    lower = jnp.concatenate([act[128:], blank], axis=0)
    upper = jnp.concatenate([blank, act[128:]], axis=0)
    for j in range(8):
        cot = sent_ref[j, :, TOK : 2 * TOK]
        rows_ref[j, :CG] = mm(cot, act[:128], 1, 1).astype(BF)
        rows_ref[j, CG:] = (mm(cot[:96], lower, 1, 1) + mm(cot[96:], upper, 1, 1)).astype(BF)


def far_kernel(
    own_ref,
    core_ref,
    sent_ref,
    other_ref,
    hidden_ref,
    pointwise_ref,
    weight_ref,
    rows_ref,
    dh_ref,
    grad_ref,
    out_ref,
    columns_ref,
):
    core, own = core_ref[0], own_ref[0]
    mine = pl.ds(pl.multiple_of(96 * core, 16), 96)
    other = pl.ds(pl.multiple_of(96 - 96 * core, 16), 96)
    for j in range(8):
        columns_ref[j, mine, :128] = sent_ref[j, :96, 2 * TOK :]
        columns_ref[j, mine, 128:] = sent_ref[j, 96:, 2 * TOK : 2 * TOK + 64]
        columns_ref[j, other, :128] = other_ref[j, :96]
        columns_ref[j, other, 128:] = other_ref[j, 96:, :64]
    hidden = hidden_ref[...]
    s = jax.nn.sigmoid(hidden)
    da = sum(mm(columns_ref[j], sent_ref[j, :, TOK : 2 * TOK], 0, 0) for j in range(8))
    dh = (da * s * (1.0 + hidden * (1.0 - s))).astype(BF)
    dh_ref[...] = dh
    back = conv_back(dh.astype(F32), weight_ref, FAR)
    grad = (sent_ref[own, :, TOK : 2 * TOK].astype(F32) + back).astype(BF)
    grad_ref[...] = grad
    for j in range(8):
        out_ref[j, :CG] = mm(pointwise_ref[j * CG : (j + 1) * CG], grad, 1, 0).astype(BF)
        for part in range(4):
            out_ref[j, CG:, 128 * part : 128 * (part + 1)] = rows_ref[j, 72 * part : 72 * (part + 1)]


def back_kernel(
    core_ref,
    got_ref,
    sent_ref,
    hidden_ref,
    start_ref,
    grad_ref,
    middle_ref,
    far_dh_ref,
    dh_ref,
    mine_ref,
    other_ref,
    far_rows_ref,
    near_rows_ref,
    seq_ref,
):
    for j in range(8):
        for part in range(4):
            seq_ref[j, 72 * part : 72 * (part + 1)] = got_ref[j, CG:, 128 * part : 128 * (part + 1)].astype(F32)
    da = sum(got_ref[j, :CG].astype(F32) for j in range(8))
    hidden = hidden_ref[...]
    s = jax.nn.sigmoid(hidden)
    dh = (da * s * (1.0 + hidden * (1.0 - s))).astype(BF)
    dh_ref[...] = dh
    conv_rows(start_ref[...].astype(F32), dh, NEAR, near_rows_ref)
    conv_rows(middle_ref[...].astype(F32), far_dh_ref[...], FAR, far_rows_ref)
    blank = jnp.zeros((8, 64), F32)
    for out_ref, core in ((mine_ref, core_ref[0]), (other_ref, 1 - core_ref[0])):
        grad = jnp.concatenate([mm(grad_ref[...], sent_ref[4 * core + j, :, :TOK], 1, 1) for j in range(4)], axis=1)
        for j in range(6):
            out_ref[CG * j : CG * (j + 1)] = grad[:, 128 * j : 128 * (j + 1)].astype(out_ref.dtype)
        rows = pl.ds(pl.multiple_of(432 * core, 8), 432)
        out_ref[1152:1584] = far_rows_ref[rows].astype(out_ref.dtype)
        out_ref[1584:2016] = near_rows_ref[rows].astype(out_ref.dtype)
        for j in range(8):
            wide = seq_ref[j, pl.ds(pl.multiple_of(96 * core, 8), 96)]
            thin = jnp.where(core == 0, seq_ref[j, CG:, :64], seq_ref[j, CG:, 64:])
            for part in range(4):
                piece = wide[24 * part : 24 * (part + 1)]
                rest = thin[24 * part : 24 * (part + 1)]
                packed = jnp.concatenate([rest[:8], rest[8:16]], axis=1), jnp.concatenate([rest[16:], blank], axis=1)
                at = 2016 + 160 * j + 40 * part
                out_ref[at : at + 40] = jnp.concatenate([piece, *packed], axis=0).astype(out_ref.dtype)


def tokens_kernel(dh_ref, weight_ref, grad_ref, out_ref):
    back = grad_ref[...].astype(F32) + conv_back(dh_ref[...].astype(F32), weight_ref, NEAR)
    rows = back.T
    out_ref[:, :16] = rows[:, :128].reshape(32, 16, 128).astype(BF)
    rest = rows[:, 128:].reshape(32, 16, 64)
    out_ref[:, 16:] = jnp.concatenate([rest[:, :8], rest[:, 8:]], axis=2).astype(BF)


def gather_kernel(mine_ref, other_ref, tokens_ref, out_ref, rows_ref):
    rows_ref[:2016] = mine_ref[:2016] + other_ref[:2016].astype(F32)
    rows_ref[2016:] = jnp.zeros((32, 128), F32)
    out_ref[:, :64] = rows_ref[...].reshape(32, 64, 128).astype(BF)
    rest = mine_ref[2016:] + other_ref[2016:].astype(F32)
    out_ref[:, 64:ROWS] = rest.reshape(32, 40, 128).astype(BF)
    out_ref[:, ROWS:] = tokens_ref[...]


def sum_kernel(got_ref, out_ref):
    total = got_ref[0, :ROWS].astype(F32)
    for j in range(1, 32):
        total = total + got_ref[j, :ROWS].astype(F32)
    piece = (total * SCALE).astype(BF)
    for j in range(32):
        out_ref[j] = piece


def finish_kernel(core_ref, mine_ref, other_ref, near_pw_ref, far_pw_ref, near_conv_ref, far_conv_ref, all_ref, far_ref):
    first = core_ref[0] == 0
    mine = mine_ref[...].astype(F32)
    other = other_ref[...].astype(F32)
    all_ref[0] = jnp.where(first, mine, other)
    all_ref[1] = jnp.where(first, other, mine)
    for j in range(12):
        for part in range(3):
            near_pw_ref[64 * part : 64 * (part + 1), 128 * j : 128 * (j + 1)] = all_ref[
                j // 6, 3 * (j % 6) + part, :64
            ].astype(BF)
    for core in range(2):
        rows = all_ref[core, 18:, :64].reshape(14 * 64, 128)
        for out_ref, at in ((far_conv_ref, 0), (near_conv_ref, 432)):
            for block in range(9):
                place = 9 * core + block
                tap, column, half = place // 6, place // 2 % 3, place % 2
                out_ref[96 * tap + 48 * half : 96 * tap + 48 * (half + 1), 128 * column : 128 * (column + 1)] = rows[
                    at + 48 * block : at + 48 * (block + 1)
                ].astype(BF)
        for part in range(4):
            at = 96 * core + 24 * part
            for pair in range(4):
                blocks = []
                for j in (2 * pair, 2 * pair + 1):
                    piece = all_ref[core, 4 * j + part, 64:ROWS]
                    rest = jnp.concatenate([piece[24:32, :64], piece[24:32, 64:], piece[32:, :64]], axis=0)
                    blocks.append((piece[:24], rest))
                (even, even_rest), (odd, odd_rest) = blocks
                col = 2 * CG * pair
                far_ref[at : at + 24, col : col + 128] = even
                far_ref[at : at + 24, col + 128 : col + 256] = jnp.concatenate([even_rest, odd[:, :64]], axis=1)
                far_ref[at : at + 24, col + 256 : col + 384] = jnp.concatenate([odd[:, 64:], odd_rest], axis=1)
    far_pw_ref[...] = far_ref[...].astype(BF)


def step(emb, order, cot, cw1, pw1, cw2, pw2):
    core = lax.axis_index("core").astype(jnp.int32).reshape(1)
    own = lax.axis_index(GRP).astype(jnp.int32).reshape(1)
    base = (lax.axis_index(SEQ) * TOK).astype(jnp.int32).reshape(1)

    (packed,) = call(pack_kernel, [((TOK, 2 * CG), BF)], (base,), (jnp.concatenate([emb, cot], axis=0),), (order.reshape(1, TOK),))
    packed = swap(packed.reshape(32, TOK // 32, 2 * CG), CHIPS).reshape(TOK, 2 * CG)
    (halves,) = call(halves_kernel, [((8, CG, 128), BF)], (core,), (), (pw2,))
    packed, own, core, w1, w2, pw1t, halves = lax.optimization_barrier(
        (packed, own, core, cw1.reshape(3, CG, CG), cw2.reshape(3, CG, CG), pw1.T, halves)
    )
    sent, near_hidden, start = call(
        near_kernel,
        [((8, CG, 2 * TOK + 128), BF), ((CG, TOK), F32), ((CG, TOK), BF)],
        (),
        (packed, w1, halves),
    )
    sent = swap(sent, GRP)
    halves = other_core(sent[:, :, 2 * TOK :])
    middle, far_hidden, pg2_rows = call(
        mid_kernel,
        [((CG, TOK), BF), ((CG, TOK), F32), ((8, CG + 96, 128), BF)],
        (),
        (sent,),
        (start, pw1t, w2),
    )
    far_dh, grad_middle, parts = call(
        far_kernel,
        [((CG, TOK), BF), ((CG, TOK), BF), ((8, CG + 72, TOK), BF)],
        (own, core),
        (sent, halves),
        (far_hidden, pw1t, w2, pg2_rows),
        scratch=[((8, CG, CG), BF)],
    )
    got = swap(parts, GRP)

    near_dh, mine, other = call(
        back_kernel,
        [((CG, TOK), BF), ((3296, 128), F32), ((3296, 128), BF)],
        (core,),
        (got, sent),
        (near_hidden, start, grad_middle, middle, far_dh),
        scratch=[((864, 128), F32), ((864, 128), F32), ((8, 288, 128), F32)],
    )
    other = other_core(other)
    (tokens,) = call(tokens_kernel, [((32, 24, 128), BF)], (), (near_dh,), (w1, grad_middle))
    (bundle,) = call(
        gather_kernel,
        [((32, ROWS + 24, 128), BF)],
        (),
        (),
        (mine, other, tokens),
        scratch=[((2048, 128), F32)],
    )
    bundle = swap(bundle, CHIPS)
    (spread,) = call(sum_kernel, [((32, ROWS, 128), BF)], (), (bundle,))
    spread = swap(spread, CHIPS)

    rest = bundle[:, ROWS + 16 :]
    rest = jnp.concatenate([rest[:, :, :64], rest[:, :, 64:]], axis=1)
    back = jnp.concatenate([bundle[:, ROWS : ROWS + 16], rest], axis=2).reshape(TOK, CG)
    onehot = (lax.broadcasted_iota(jnp.int32, (TOK, TOK), 0) == (order - base)[None, :]).astype(BF)
    emb_grad = mm(back, onehot, 0, 1).astype(BF)

    out_pg1, out_pg2, out_cg1, out_cg2 = call(
        finish_kernel,
        [((CG, 8 * CG), BF), ((CG, 8 * CG), BF), ((288, 384), BF), ((288, 384), BF)],
        (core,),
        (spread, other_core(spread)),
        scratch=[((2, 32, ROWS, 128), F32), ((CG, 8 * CG), F32)],
        mib=12,
    )
    flat = (1, 3 * CG * CG)
    return emb_grad, out_cg1.reshape(flat), out_pg1, out_cg2.reshape(flat), out_pg2


def solution(mesh):
    fine = Mesh(mesh.devices.reshape(4, 4, 2, 2, 4, 2), SEQ + GRP)
    placed = (P(GRP, SEQ), P(SEQ), P(GRP, SEQ), P(GRP, None), P(GRP, None), P(GRP, None), P(GRP, None))
    return jax.shard_map(
        step,
        mesh=fine,
        in_specs=placed,
        out_specs=(P(GRP, SEQ), P(GRP, None), P(GRP, None), P(GRP, None), P(GRP, None)),
        check_vma=False,
    )
```

```python
import jax
import jax.numpy as jnp
from jax import lax
from jax.experimental import pallas as pl
from jax.experimental.pallas import tpu as pltpu
from jax.sharding import Mesh, PartitionSpec as P

CG = 192
TOK = 512
NEAR = 32
FAR = 64
BF = jnp.bfloat16
F32 = jnp.float32
SEQ = ("zh", "yh", "yl", "core")
GRP = ("x", "zl")
CHIPS = ("zh", "yh", "yl")
SCALE = float(32768) ** (-0.5)
ROWS = 104


def mm(a, b, ca, cb):
    return lax.dot_general(a, b, (((ca,), (cb,)), ((), ())), preferred_element_type=F32)


def swap(blocks, axes):
    return lax.all_to_all(blocks, axes, 0, 0, tiled=True)


def other_core(values):
    return lax.ppermute(values, "core", [(0, 1), (1, 0)])


def call(kernel, outs, scalars, direct, fetched=(), scratch=(), mib=8, space=pl.ANY, flops=0):
    vmem = pl.BlockSpec(memory_space=pltpu.VMEM)
    smem = pl.BlockSpec(memory_space=pltpu.SMEM)
    anywhere = pl.BlockSpec(memory_space=space)
    n_near, n_far, n_out = len(scalars) + len(direct), len(fetched), len(outs)

    def body(*refs):
        near, far, out, rest = (
            refs[:n_near],
            refs[n_near : n_near + n_far],
            refs[n_near + n_far : n_near + n_far + n_out],
            refs[n_near + n_far + n_out :],
        )
        buffers, own = rest[:n_far], rest[n_far:]
        if n_far:
            sems, own = own[-1], own[:-1]
            copies = [pltpu.make_async_copy(far[i], buffers[i], sems.at[i]) for i in range(n_far)]
            for copy in copies:
                copy.start()
            for copy in copies:
                copy.wait()
        kernel(*near, *buffers, *out, *own)

    return pl.pallas_call(
        body,
        out_shape=[jax.ShapeDtypeStruct(shape, dtype) for shape, dtype in outs],
        in_specs=[smem] * len(scalars) + [vmem] * len(direct) + [anywhere] * n_far,
        out_specs=[vmem] * n_out,
        scratch_shapes=[pltpu.VMEM(x.shape, x.dtype) for x in fetched]
        + [pltpu.VMEM(shape, dtype) for shape, dtype in scratch]
        + ([pltpu.SemaphoreType.DMA((n_far,))] if n_far else []),
        compiler_params=pltpu.CompilerParams(vmem_limit_bytes=mib * 1024 * 1024),
        cost_estimate=pl.CostEstimate(flops=flops, bytes_accessed=0, transcendentals=0) if flops else None,
    )(*scalars, *direct, *fetched)


def shifted(values, by):
    if by == 0:
        return values.astype(BF)
    lane = lax.broadcasted_iota(jnp.int32, values.shape, 1)
    rolled = pltpu.roll(values, (-by) % TOK, 1)
    keep = lane < TOK - by if by > 0 else lane >= -by
    return jnp.where(keep, rolled, 0.0).astype(BF)


def conv_back(grads, weight_ref, by):
    return (
        mm(weight_ref[0], shifted(grads, by), 1, 0)
        + mm(weight_ref[1], shifted(grads, 0), 1, 0)
        + mm(weight_ref[2], shifted(grads, -by), 1, 0)
    )


def conv_rows(values, grads, by, rows_ref):
    row = lax.broadcasted_iota(jnp.int32, (CG, CG), 0)
    col = lax.broadcasted_iota(jnp.int32, (CG, CG), 1)
    half = CG // 2
    source = jnp.where(row < half, 2 * row, 2 * row - (CG - 1))
    order = jnp.where(col == source, 1.0, 0.0).astype(BF)
    for tap, distance in enumerate((-by, 0, by)):
        moved = mm(order, shifted(values, distance), 1, 0).astype(BF)
        grad = mm(moved, grads, 1, 1)
        even, odd = grad[:half], grad[half:]
        base = 3 * half * tap
        rows_ref[base : base + half] = even[:, :128]
        rows_ref[base + half : base + 2 * half] = jnp.concatenate([even[:, 128:], odd[:, :64]], axis=1)
        rows_ref[base + 2 * half : base + 3 * half] = odd[:, 64:]


def pack_kernel(base_ref, both_ref, order_ref, out_ref):
    token = lax.broadcasted_iota(jnp.int32, (TOK, TOK), 0)
    onehot = jnp.where(token == order_ref[...] - base_ref[0], 1.0, 0.0).astype(BF)
    start = mm(both_ref[:CG], onehot, 1, 0)
    both = jnp.concatenate([start, both_ref[CG:].astype(F32)], axis=0)
    out_ref[...] = both.T.astype(BF)


def halves_kernel(core_ref, weight_ref, out_ref):
    half = weight_ref[pl.ds(pl.multiple_of(96 * core_ref[0], 16), 96)].astype(F32)
    blank = jnp.zeros((96, 64), F32)
    for j in range(8):
        block = half[:, CG * j : CG * (j + 1)]
        out_ref[j, :96] = block[:, :128].astype(BF)
        out_ref[j, 96:] = jnp.concatenate([block[:, 128:], blank], axis=1).astype(BF)


def near_kernel(tokens_ref, weight_ref, blocks_ref, out_ref, hidden_ref, start_ref):
    rows = tokens_ref[...].astype(F32)
    both = rows.T
    start_ref[...] = both[:CG].astype(BF)
    cot = both[CG:].astype(BF)
    start = rows[:, :CG]
    filler = jnp.zeros((NEAR, CG), F32)
    before = jnp.concatenate([filler, start[: TOK - NEAR]], axis=0).astype(BF)
    after = jnp.concatenate([start[NEAR:], filler], axis=0).astype(BF)
    hidden = (
        mm(weight_ref[0], before, 0, 1)
        + mm(weight_ref[1], start.astype(BF), 0, 1)
        + mm(weight_ref[2], after, 0, 1)
    )
    hidden_ref[...] = hidden
    act = (hidden * jax.nn.sigmoid(hidden)).astype(BF)
    for j in range(8):
        out_ref[j, :, :TOK] = act
        out_ref[j, :, TOK : 2 * TOK] = cot
        out_ref[j, :, 2 * TOK :] = blocks_ref[j]


def mid_kernel(
    core_ref, sent_ref, start_ref, pointwise_ref, weight_ref, middle_ref, hidden_ref, mine_ref, other_ref
):
    middle = start_ref[...].astype(F32) + sum(
        mm(pointwise_ref[j * CG : (j + 1) * CG], sent_ref[j, :, :TOK], 0, 0) for j in range(8)
    )
    middle = middle.astype(BF)
    middle_ref[...] = middle
    wide = middle.astype(F32)
    hidden = (
        mm(weight_ref[0], shifted(wide, -FAR), 0, 0)
        + mm(weight_ref[1], middle, 0, 0)
        + mm(weight_ref[2], shifted(wide, FAR), 0, 0)
    )
    hidden_ref[...] = hidden
    act = (hidden * jax.nn.sigmoid(hidden)).astype(BF)
    blank = jnp.zeros((64, TOK), BF)
    lower = jnp.concatenate([act[128:], blank], axis=0)
    upper = jnp.concatenate([blank, act[128:]], axis=0)
    for j in range(8):
        other_ref[j, :CG] = sent_ref[j, :, 2 * TOK :]
        for out_ref, at, core in ((mine_ref, 0, core_ref[0]), (other_ref, CG, 1 - core_ref[0])):
            cot = sent_ref[j, pl.ds(pl.multiple_of(96 * core, 16), 96), TOK : 2 * TOK]
            wide = mm(cot, act[:128], 1, 1)
            thin = mm(cot[:48], lower, 1, 1) + mm(cot[48:], upper, 1, 1)
            for part in range(4):
                row = at + 40 * part
                rest = thin[16 * part : 16 * (part + 1)] if part < 3 else jnp.zeros((16, 128), F32)
                piece = jnp.concatenate([wide[24 * part : 24 * (part + 1)], rest], axis=0)
                out_ref[j, row : row + 40] = piece.astype(out_ref.dtype)


def far_kernel(
    own_ref,
    core_ref,
    sent_ref,
    other_ref,
    hidden_ref,
    pointwise_ref,
    weight_ref,
    rows_ref,
    dh_ref,
    grad_ref,
    out_ref,
    columns_ref,
):
    core, own = core_ref[0], own_ref[0]
    mine = pl.ds(pl.multiple_of(96 * core, 16), 96)
    other = pl.ds(pl.multiple_of(96 - 96 * core, 16), 96)
    for j in range(8):
        columns_ref[j, mine, :128] = sent_ref[j, :96, 2 * TOK :]
        columns_ref[j, mine, 128:] = sent_ref[j, 96:, 2 * TOK : 2 * TOK + 64]
        columns_ref[j, other, :128] = other_ref[j, :96]
        columns_ref[j, other, 128:] = other_ref[j, 96:CG, :64]
    hidden = hidden_ref[...]
    s = jax.nn.sigmoid(hidden)
    da = sum(mm(columns_ref[j], sent_ref[j, :, TOK : 2 * TOK], 0, 0) for j in range(8))
    dh = (da * s * (1.0 + hidden * (1.0 - s))).astype(BF)
    dh_ref[...] = dh
    back = conv_back(dh.astype(F32), weight_ref, FAR)
    grad = (sent_ref[own, :, TOK : 2 * TOK].astype(F32) + back).astype(BF)
    grad_ref[...] = grad
    for j in range(8):
        out_ref[j, :CG] = mm(pointwise_ref[j * CG : (j + 1) * CG], grad, 1, 0).astype(BF)
        for part in range(4):
            rows = slice(40 * part, 40 * (part + 1))
            theirs = other_ref[j, CG + 40 * part : CG + 40 * (part + 1)].astype(F32)
            out_ref[j, CG:, 128 * part : 128 * (part + 1)] = (rows_ref[j, rows] + theirs).astype(BF)


def columns_of(grad, sent_ref, core, out_ref):
    half = jnp.concatenate([mm(grad, sent_ref[4 * core + j, :, :TOK], 1, 1) for j in range(4)], axis=1)
    for j in range(6):
        out_ref[CG * j : CG * (j + 1)] = half[:, 128 * j : 128 * (j + 1)].astype(out_ref.dtype)


def back_kernel(
    core_ref,
    got_ref,
    sent_ref,
    hidden_ref,
    start_ref,
    grad_ref,
    middle_ref,
    far_dh_ref,
    dh_ref,
    mine_ref,
    other_ref,
    far_rows_ref,
    near_rows_ref,
):
    core = core_ref[0]
    da = sum(got_ref[j, :CG].astype(F32) for j in range(8))
    hidden = hidden_ref[...]
    s = jax.nn.sigmoid(hidden)
    dh = (da * s * (1.0 + hidden * (1.0 - s))).astype(BF)
    dh_ref[...] = dh
    conv_rows(start_ref[...].astype(F32), dh, NEAR, near_rows_ref)
    conv_rows(middle_ref[...].astype(F32), far_dh_ref[...], FAR, far_rows_ref)
    mine = pl.ds(pl.multiple_of(432 * core, 8), 432)
    mine_ref[:432] = far_rows_ref[mine]
    mine_ref[432:] = near_rows_ref[mine]
    other = pl.ds(pl.multiple_of(432 - 432 * core, 8), 432)
    other_ref[1152:1584] = far_rows_ref[other].astype(BF)
    other_ref[1584:] = near_rows_ref[other].astype(BF)
    columns_of(grad_ref[...], sent_ref, 1 - core, other_ref)


def keep_kernel(core_ref, sent_ref, dh_ref, weight_ref, grad_ref, mine_ref, out_ref):
    columns_of(grad_ref[...], sent_ref, core_ref[0], mine_ref)
    back = grad_ref[...].astype(F32) + conv_back(dh_ref[...].astype(F32), weight_ref, NEAR)
    rows = back.T
    out_ref[:, :16] = rows[:, :128].reshape(32, 16, 128).astype(BF)
    rest = rows[:, 128:].reshape(32, 16, 64)
    out_ref[:, 16:] = jnp.concatenate([rest[:, :8], rest[:, 8:]], axis=2).astype(BF)


def gather_kernel(got_ref, columns_ref, conv_ref, other_ref, tokens_ref, out_ref, rows_ref):
    rows_ref[:1152] = columns_ref[...] + other_ref[:1152].astype(F32)
    rows_ref[1152:2016] = conv_ref[...] + other_ref[1152:].astype(F32)
    rows_ref[2016:] = jnp.zeros((32, 128), F32)
    out_ref[:, :64] = rows_ref[...].reshape(32, 64, 128).astype(BF)
    for j in range(8):
        for part in range(4):
            out_ref[4 * j + part, 64:ROWS] = got_ref[j, CG:, 128 * part : 128 * (part + 1)]
    out_ref[:, ROWS:] = tokens_ref[...]


def sum_kernel(got_ref, out_ref):
    total = got_ref[0, :ROWS].astype(F32)
    for j in range(1, 32):
        total = total + got_ref[j, :ROWS].astype(F32)
    piece = (total * SCALE).astype(BF)
    for j in range(32):
        out_ref[j] = piece


def finish_kernel(core_ref, mine_ref, other_ref, near_pw_ref, far_pw_ref, near_conv_ref, far_conv_ref, all_ref, far_ref):
    first = core_ref[0] == 0
    mine = mine_ref[...].astype(F32)
    other = other_ref[...].astype(F32)
    all_ref[0] = jnp.where(first, mine, other)
    all_ref[1] = jnp.where(first, other, mine)
    for j in range(12):
        for part in range(3):
            near_pw_ref[64 * part : 64 * (part + 1), 128 * j : 128 * (j + 1)] = all_ref[
                j // 6, 3 * (j % 6) + part, :64
            ].astype(BF)
    for core in range(2):
        rows = all_ref[core, 18:, :64].reshape(14 * 64, 128)
        for out_ref, at in ((far_conv_ref, 0), (near_conv_ref, 432)):
            for block in range(9):
                place = 9 * core + block
                tap, column, half = place // 6, place // 2 % 3, place % 2
                out_ref[96 * tap + 48 * half : 96 * tap + 48 * (half + 1), 128 * column : 128 * (column + 1)] = rows[
                    at + 48 * block : at + 48 * (block + 1)
                ].astype(BF)
        at = 96 * core
        for pair in range(4):
            blocks = []
            for j in (2 * pair, 2 * pair + 1):
                pieces = [all_ref[core, 4 * j + part, 64:ROWS] for part in range(4)]
                rest = jnp.concatenate([piece[24:] for piece in pieces[:3]], axis=0)
                wide = jnp.concatenate([piece[:24] for piece in pieces], axis=0)
                blocks.append((wide, jnp.concatenate([rest[:, :64], rest[:, 64:]], axis=0)))
            (even, even_rest), (odd, odd_rest) = blocks
            col = 2 * CG * pair
            far_ref[at : at + 96, col : col + 128] = even
            far_ref[at : at + 96, col + 128 : col + 256] = jnp.concatenate([even_rest, odd[:, :64]], axis=1)
            far_ref[at : at + 96, col + 256 : col + 384] = jnp.concatenate([odd[:, 64:], odd_rest], axis=1)
    far_pw_ref[...] = far_ref[...].astype(BF)


def step(emb, order, cot, cw1, pw1, cw2, pw2):
    core = lax.axis_index("core").astype(jnp.int32).reshape(1)
    own = lax.axis_index(GRP).astype(jnp.int32).reshape(1)
    base = (lax.axis_index(SEQ) * TOK).astype(jnp.int32).reshape(1)

    both = jnp.concatenate([emb, cot], axis=0)
    (packed,) = call(pack_kernel, [((TOK, 2 * CG), BF)], (base,), (both,), (order.reshape(1, TOK),))
    packed = swap(packed.reshape(32, TOK // 32, 2 * CG), CHIPS).reshape(TOK, 2 * CG)
    (halves,) = call(halves_kernel, [((8, CG, 128), BF)], (core,), (), (pw2,))
    packed, own, core, w1, w2, pw1t, halves = lax.optimization_barrier(
        (packed, own, core, cw1.reshape(3, CG, CG), cw2.reshape(3, CG, CG), pw1.T, halves)
    )
    sent, near_hidden, start = call(
        near_kernel,
        [((8, CG, 2 * TOK + 128), BF), ((CG, TOK), F32), ((CG, TOK), BF)],
        (),
        (packed, w1, halves),
    )
    sent = swap(sent, GRP)
    middle, far_hidden, pg2_mine, halves = call(
        mid_kernel,
        [((CG, TOK), BF), ((CG, TOK), F32), ((8, 160, 128), F32), ((8, CG + 160, 128), BF)],
        (core,),
        (sent,),
        (start, pw1t, w2),
    )
    halves = other_core(halves)
    far_dh, grad_middle, parts = call(
        far_kernel,
        [((CG, TOK), BF), ((CG, TOK), BF), ((8, CG + 40, TOK), BF)],
        (own, core),
        (sent, halves),
        (far_hidden, pw1t, w2, pg2_mine),
        scratch=[((8, CG, CG), BF)],
    )
    got = swap(parts, GRP)

    near_dh, conv_mine, other = call(
        back_kernel,
        [((CG, TOK), BF), ((864, 128), F32), ((2016, 128), BF)],
        (core,),
        (got, sent),
        (near_hidden, start, grad_middle, middle, far_dh),
        scratch=[((864, 128), F32), ((864, 128), F32)],
    )
    other = other_core(other)
    pg1_mine, tokens = call(
        keep_kernel,
        [((1152, 128), F32), ((32, 24, 128), BF)],
        (core,),
        (sent, near_dh),
        (w1, grad_middle),
    )
    (bundle,) = call(
        gather_kernel,
        [((32, ROWS + 24, 128), BF)],
        (),
        (got,),
        (pg1_mine, conv_mine, other, tokens),
        scratch=[((2048, 128), F32)],
    )
    bundle = swap(bundle, CHIPS)
    (spread,) = call(sum_kernel, [((32, ROWS, 128), BF)], (), (bundle,))
    spread = swap(spread, CHIPS)

    rest = bundle[:, ROWS + 16 :]
    rest = jnp.concatenate([rest[:, :, :64], rest[:, :, 64:]], axis=1)
    back = jnp.concatenate([bundle[:, ROWS : ROWS + 16], rest], axis=2).reshape(TOK, CG)
    onehot = (lax.broadcasted_iota(jnp.int32, (TOK, TOK), 0) == (order - base)[None, :]).astype(BF)
    emb_grad = mm(back, onehot, 0, 1).astype(BF)

    out_pg1, out_pg2, out_cg1, out_cg2 = call(
        finish_kernel,
        [((CG, 8 * CG), BF), ((CG, 8 * CG), BF), ((288, 384), BF), ((288, 384), BF)],
        (core,),
        (spread, other_core(spread)),
        scratch=[((2, 32, ROWS, 128), F32), ((CG, 8 * CG), F32)],
        mib=12,
    )
    flat = (1, 3 * CG * CG)
    return emb_grad, out_cg1.reshape(flat), out_pg1, out_cg2.reshape(flat), out_pg2


def solution(mesh):
    fine = Mesh(mesh.devices.reshape(4, 4, 2, 2, 4, 2), SEQ + GRP)
    placed = (P(GRP, SEQ), P(SEQ), P(GRP, SEQ), P(GRP, None), P(GRP, None), P(GRP, None), P(GRP, None))
    return jax.shard_map(
        step,
        mesh=fine,
        in_specs=placed,
        out_specs=(P(GRP, SEQ), P(GRP, None), P(GRP, None), P(GRP, None), P(GRP, None)),
        check_vma=False,
    )
```

```python
import jax
import jax.numpy as jnp
from jax import lax
from jax.experimental import pallas as pl
from jax.experimental.pallas import tpu as pltpu
from jax.sharding import Mesh, PartitionSpec as P

CG = 192
TOK = 512
NEAR = 32
FAR = 64
BF = jnp.bfloat16
F32 = jnp.float32
SEQ = ("zh", "yh", "yl", "core")
GRP = ("x", "zl")
CHIPS = ("zh", "yh", "yl")
SCALE = float(32768) ** (-0.5)
ROWS = 104


def mm(a, b, ca, cb):
    return lax.dot_general(a, b, (((ca,), (cb,)), ((), ())), preferred_element_type=F32)


def swap(blocks, axes):
    return lax.all_to_all(blocks, axes, 0, 0, tiled=True)


def other_core(values):
    return lax.ppermute(values, "core", [(0, 1), (1, 0)])


def call(kernel, outs, scalars, direct, fetched=(), scratch=(), mib=8, space=pl.ANY, flops=0):
    vmem = pl.BlockSpec(memory_space=pltpu.VMEM)
    smem = pl.BlockSpec(memory_space=pltpu.SMEM)
    anywhere = pl.BlockSpec(memory_space=space)
    n_near, n_far, n_out = len(scalars) + len(direct), len(fetched), len(outs)

    def body(*refs):
        near, far, out, rest = (
            refs[:n_near],
            refs[n_near : n_near + n_far],
            refs[n_near + n_far : n_near + n_far + n_out],
            refs[n_near + n_far + n_out :],
        )
        buffers, own = rest[:n_far], rest[n_far:]
        if n_far:
            sems, own = own[-1], own[:-1]
            copies = [pltpu.make_async_copy(far[i], buffers[i], sems.at[i]) for i in range(n_far)]
            for copy in copies:
                copy.start()
            for copy in copies:
                copy.wait()
        kernel(*near, *buffers, *out, *own)

    return pl.pallas_call(
        body,
        out_shape=[jax.ShapeDtypeStruct(shape, dtype) for shape, dtype in outs],
        in_specs=[smem] * len(scalars) + [vmem] * len(direct) + [anywhere] * n_far,
        out_specs=[vmem] * n_out,
        scratch_shapes=[pltpu.VMEM(x.shape, x.dtype) for x in fetched]
        + [pltpu.VMEM(shape, dtype) for shape, dtype in scratch]
        + ([pltpu.SemaphoreType.DMA((n_far,))] if n_far else []),
        compiler_params=pltpu.CompilerParams(vmem_limit_bytes=mib * 1024 * 1024),
        cost_estimate=pl.CostEstimate(flops=flops, bytes_accessed=0, transcendentals=0) if flops else None,
    )(*scalars, *direct, *fetched)


def shifted(values, by):
    if by == 0:
        return values.astype(BF)
    lane = lax.broadcasted_iota(jnp.int32, values.shape, 1)
    rolled = pltpu.roll(values, (-by) % TOK, 1)
    keep = lane < TOK - by if by > 0 else lane >= -by
    return jnp.where(keep, rolled, 0.0).astype(BF)


def conv_back(grads, weight_ref, by):
    return (
        mm(weight_ref[0], shifted(grads, by), 1, 0)
        + mm(weight_ref[1], shifted(grads, 0), 1, 0)
        + mm(weight_ref[2], shifted(grads, -by), 1, 0)
    )


def conv_rows(values, grads, by, rows_ref):
    row = lax.broadcasted_iota(jnp.int32, (CG, CG), 0)
    col = lax.broadcasted_iota(jnp.int32, (CG, CG), 1)
    half = CG // 2
    source = jnp.where(row < half, 2 * row, 2 * row - (CG - 1))
    order = jnp.where(col == source, 1.0, 0.0).astype(BF)
    for tap, distance in enumerate((-by, 0, by)):
        moved = mm(order, shifted(values, distance), 1, 0).astype(BF)
        grad = mm(moved, grads, 1, 1)
        even, odd = grad[:half], grad[half:]
        base = 3 * half * tap
        rows_ref[base : base + half] = even[:, :128]
        rows_ref[base + half : base + 2 * half] = jnp.concatenate([even[:, 128:], odd[:, :64]], axis=1)
        rows_ref[base + 2 * half : base + 3 * half] = odd[:, 64:]


def pack_kernel(base_ref, both_ref, order_ref, out_ref):
    token = lax.broadcasted_iota(jnp.int32, (TOK, TOK), 0)
    onehot = jnp.where(token == order_ref[...] - base_ref[0], 1.0, 0.0).astype(BF)
    start = mm(both_ref[:CG], onehot, 1, 0)
    both = jnp.concatenate([start, both_ref[CG:].astype(F32)], axis=0)
    out_ref[...] = both.T.astype(BF)


def halves_kernel(core_ref, weight_ref, out_ref):
    half = weight_ref[pl.ds(pl.multiple_of(96 * core_ref[0], 16), 96)].astype(F32)
    blank = jnp.zeros((96, 64), F32)
    for j in range(8):
        block = half[:, CG * j : CG * (j + 1)]
        out_ref[j, :96] = block[:, :128].astype(BF)
        out_ref[j, 96:] = jnp.concatenate([block[:, 128:], blank], axis=1).astype(BF)


def near_kernel(tokens_ref, weight_ref, blocks_ref, out_ref, hidden_ref, start_ref):
    rows = tokens_ref[...].astype(F32)
    both = rows.T
    start_ref[...] = both[:CG].astype(BF)
    cot = both[CG:].astype(BF)
    start = rows[:, :CG]
    filler = jnp.zeros((NEAR, CG), F32)
    before = jnp.concatenate([filler, start[: TOK - NEAR]], axis=0).astype(BF)
    after = jnp.concatenate([start[NEAR:], filler], axis=0).astype(BF)
    hidden = (
        mm(weight_ref[0], before, 0, 1)
        + mm(weight_ref[1], start.astype(BF), 0, 1)
        + mm(weight_ref[2], after, 0, 1)
    )
    hidden_ref[...] = hidden
    act = (hidden * jax.nn.sigmoid(hidden)).astype(BF)
    for j in range(8):
        out_ref[j, :, :TOK] = act
        out_ref[j, :, TOK : 2 * TOK] = cot
        out_ref[j, :, 2 * TOK :] = blocks_ref[j]


def mid_kernel(
    core_ref, sent_ref, start_ref, pointwise_ref, weight_ref, middle_ref, hidden_ref, act_ref, other_ref
):
    middle = start_ref[...].astype(F32) + sum(
        mm(pointwise_ref[j * CG : (j + 1) * CG], sent_ref[j, :, :TOK], 0, 0) for j in range(8)
    )
    middle = middle.astype(BF)
    middle_ref[...] = middle
    wide = middle.astype(F32)
    hidden = (
        mm(weight_ref[0], shifted(wide, -FAR), 0, 0)
        + mm(weight_ref[1], middle, 0, 0)
        + mm(weight_ref[2], shifted(wide, FAR), 0, 0)
    )
    hidden_ref[...] = hidden
    act = (hidden * jax.nn.sigmoid(hidden)).astype(BF)
    act_ref[...] = act
    for j in range(8):
        other_ref[j, :CG] = sent_ref[j, :, 2 * TOK :]
    block_of(act, sent_ref, 1 - core_ref[0], other_ref, CG)


def block_of(act, sent_ref, core, out_ref, at):
    blank = jnp.zeros((64, TOK), BF)
    lower = jnp.concatenate([act[128:], blank], axis=0)
    upper = jnp.concatenate([blank, act[128:]], axis=0)
    for j in range(8):
        cot = sent_ref[j, pl.ds(pl.multiple_of(96 * core, 16), 96), TOK : 2 * TOK]
        wide = mm(cot, act[:128], 1, 1)
        thin = mm(cot[:48], lower, 1, 1) + mm(cot[48:], upper, 1, 1)
        for part in range(4):
            row = at + 40 * part
            rest = thin[16 * part : 16 * (part + 1)] if part < 3 else jnp.zeros((16, 128), F32)
            piece = jnp.concatenate([wide[24 * part : 24 * (part + 1)], rest], axis=0)
            out_ref[j, row : row + 40] = piece.astype(out_ref.dtype)


def block_kernel(core_ref, sent_ref, act_ref, mine_ref):
    block_of(act_ref[...], sent_ref, core_ref[0], mine_ref, 0)


def far_kernel(
    own_ref,
    core_ref,
    sent_ref,
    other_ref,
    hidden_ref,
    pointwise_ref,
    weight_ref,
    rows_ref,
    dh_ref,
    grad_ref,
    out_ref,
    columns_ref,
):
    core, own = core_ref[0], own_ref[0]
    mine = pl.ds(pl.multiple_of(96 * core, 16), 96)
    other = pl.ds(pl.multiple_of(96 - 96 * core, 16), 96)
    for j in range(8):
        columns_ref[j, mine, :128] = sent_ref[j, :96, 2 * TOK :]
        columns_ref[j, mine, 128:] = sent_ref[j, 96:, 2 * TOK : 2 * TOK + 64]
        columns_ref[j, other, :128] = other_ref[j, :96]
        columns_ref[j, other, 128:] = other_ref[j, 96:CG, :64]
    hidden = hidden_ref[...]
    s = jax.nn.sigmoid(hidden)
    da = sum(mm(columns_ref[j], sent_ref[j, :, TOK : 2 * TOK], 0, 0) for j in range(8))
    dh = (da * s * (1.0 + hidden * (1.0 - s))).astype(BF)
    dh_ref[...] = dh
    back = conv_back(dh.astype(F32), weight_ref, FAR)
    grad = (sent_ref[own, :, TOK : 2 * TOK].astype(F32) + back).astype(BF)
    grad_ref[...] = grad
    for j in range(8):
        out_ref[j, :CG] = mm(pointwise_ref[j * CG : (j + 1) * CG], grad, 1, 0).astype(BF)
        for part in range(4):
            rows = slice(40 * part, 40 * (part + 1))
            theirs = other_ref[j, CG + 40 * part : CG + 40 * (part + 1)].astype(F32)
            out_ref[j, CG:, 128 * part : 128 * (part + 1)] = (rows_ref[j, rows] + theirs).astype(BF)


def columns_of(grad, sent_ref, core, out_ref):
    half = jnp.concatenate([mm(grad, sent_ref[4 * core + j, :, :TOK], 1, 1) for j in range(4)], axis=1)
    for j in range(6):
        out_ref[CG * j : CG * (j + 1)] = half[:, 128 * j : 128 * (j + 1)].astype(out_ref.dtype)


def back_kernel(
    core_ref,
    got_ref,
    sent_ref,
    hidden_ref,
    start_ref,
    grad_ref,
    middle_ref,
    far_dh_ref,
    dh_ref,
    mine_ref,
    other_ref,
    far_rows_ref,
    near_rows_ref,
):
    core = core_ref[0]
    da = sum(got_ref[j, :CG].astype(F32) for j in range(8))
    hidden = hidden_ref[...]
    s = jax.nn.sigmoid(hidden)
    dh = (da * s * (1.0 + hidden * (1.0 - s))).astype(BF)
    dh_ref[...] = dh
    conv_rows(start_ref[...].astype(F32), dh, NEAR, near_rows_ref)
    conv_rows(middle_ref[...].astype(F32), far_dh_ref[...], FAR, far_rows_ref)
    mine = pl.ds(pl.multiple_of(432 * core, 8), 432)
    mine_ref[:432] = far_rows_ref[mine]
    mine_ref[432:] = near_rows_ref[mine]
    other = pl.ds(pl.multiple_of(432 - 432 * core, 8), 432)
    other_ref[1152:1584] = far_rows_ref[other].astype(BF)
    other_ref[1584:] = near_rows_ref[other].astype(BF)
    columns_of(grad_ref[...], sent_ref, 1 - core, other_ref)


def keep_kernel(core_ref, sent_ref, dh_ref, weight_ref, grad_ref, mine_ref, out_ref):
    columns_of(grad_ref[...], sent_ref, core_ref[0], mine_ref)
    back = grad_ref[...].astype(F32) + conv_back(dh_ref[...].astype(F32), weight_ref, NEAR)
    rows = back.T
    out_ref[:, :16] = rows[:, :128].reshape(32, 16, 128).astype(BF)
    rest = rows[:, 128:].reshape(32, 16, 64)
    out_ref[:, 16:] = jnp.concatenate([rest[:, :8], rest[:, 8:]], axis=2).astype(BF)


def gather_kernel(got_ref, columns_ref, conv_ref, other_ref, tokens_ref, out_ref, rows_ref):
    rows_ref[:1152] = columns_ref[...] + other_ref[:1152].astype(F32)
    rows_ref[1152:2016] = conv_ref[...] + other_ref[1152:].astype(F32)
    rows_ref[2016:] = jnp.zeros((32, 128), F32)
    out_ref[:, :64] = rows_ref[...].reshape(32, 64, 128).astype(BF)
    for j in range(8):
        for part in range(4):
            out_ref[4 * j + part, 64:ROWS] = got_ref[j, CG:, 128 * part : 128 * (part + 1)]
    out_ref[:, ROWS:] = tokens_ref[...]


def sum_kernel(got_ref, out_ref):
    total = got_ref[0, :ROWS].astype(F32)
    for j in range(1, 32):
        total = total + got_ref[j, :ROWS].astype(F32)
    piece = (total * SCALE).astype(BF)
    for j in range(32):
        out_ref[j] = piece


def finish_kernel(core_ref, mine_ref, other_ref, near_pw_ref, far_pw_ref, near_conv_ref, far_conv_ref, all_ref, far_ref):
    first = core_ref[0] == 0
    mine = mine_ref[...].astype(F32)
    other = other_ref[...].astype(F32)
    all_ref[0] = jnp.where(first, mine, other)
    all_ref[1] = jnp.where(first, other, mine)
    for j in range(12):
        for part in range(3):
            near_pw_ref[64 * part : 64 * (part + 1), 128 * j : 128 * (j + 1)] = all_ref[
                j // 6, 3 * (j % 6) + part, :64
            ].astype(BF)
    for core in range(2):
        rows = all_ref[core, 18:, :64].reshape(14 * 64, 128)
        for out_ref, at in ((far_conv_ref, 0), (near_conv_ref, 432)):
            for block in range(9):
                place = 9 * core + block
                tap, column, half = place // 6, place // 2 % 3, place % 2
                out_ref[96 * tap + 48 * half : 96 * tap + 48 * (half + 1), 128 * column : 128 * (column + 1)] = rows[
                    at + 48 * block : at + 48 * (block + 1)
                ].astype(BF)
        at = 96 * core
        for pair in range(4):
            blocks = []
            for j in (2 * pair, 2 * pair + 1):
                pieces = [all_ref[core, 4 * j + part, 64:ROWS] for part in range(4)]
                rest = jnp.concatenate([piece[24:] for piece in pieces[:3]], axis=0)
                wide = jnp.concatenate([piece[:24] for piece in pieces], axis=0)
                blocks.append((wide, jnp.concatenate([rest[:, :64], rest[:, 64:]], axis=0)))
            (even, even_rest), (odd, odd_rest) = blocks
            col = 2 * CG * pair
            far_ref[at : at + 96, col : col + 128] = even
            far_ref[at : at + 96, col + 128 : col + 256] = jnp.concatenate([even_rest, odd[:, :64]], axis=1)
            far_ref[at : at + 96, col + 256 : col + 384] = jnp.concatenate([odd[:, 64:], odd_rest], axis=1)
    far_pw_ref[...] = far_ref[...].astype(BF)


def step(emb, order, cot, cw1, pw1, cw2, pw2):
    core = lax.axis_index("core").astype(jnp.int32).reshape(1)
    own = lax.axis_index(GRP).astype(jnp.int32).reshape(1)
    base = (lax.axis_index(SEQ) * TOK).astype(jnp.int32).reshape(1)

    both = jnp.concatenate([emb, cot], axis=0)
    (packed,) = call(pack_kernel, [((TOK, 2 * CG), BF)], (base,), (both,), (order.reshape(1, TOK),))
    packed = swap(packed.reshape(32, TOK // 32, 2 * CG), CHIPS).reshape(TOK, 2 * CG)
    (halves,) = call(halves_kernel, [((8, CG, 128), BF)], (core,), (), (pw2,))
    packed, own, core, w1, w2, pw1t, halves = lax.optimization_barrier(
        (packed, own, core, cw1.reshape(3, CG, CG), cw2.reshape(3, CG, CG), pw1.T, halves)
    )
    sent, near_hidden, start = call(
        near_kernel,
        [((8, CG, 2 * TOK + 128), BF), ((CG, TOK), F32), ((CG, TOK), BF)],
        (),
        (packed, w1, halves),
    )
    sent = swap(sent, GRP)
    middle, far_hidden, far_act, halves = call(
        mid_kernel,
        [((CG, TOK), BF), ((CG, TOK), F32), ((CG, TOK), BF), ((8, CG + 160, 128), BF)],
        (core,),
        (sent,),
        (start, pw1t, w2),
    )
    halves = other_core(halves)
    (pg2_mine,) = call(block_kernel, [((8, 160, 128), F32)], (core,), (sent, far_act))
    far_dh, grad_middle, parts = call(
        far_kernel,
        [((CG, TOK), BF), ((CG, TOK), BF), ((8, CG + 40, TOK), BF)],
        (own, core),
        (sent, halves),
        (far_hidden, pw1t, w2, pg2_mine),
        scratch=[((8, CG, CG), BF)],
    )
    got = swap(parts, GRP)

    near_dh, conv_mine, other = call(
        back_kernel,
        [((CG, TOK), BF), ((864, 128), F32), ((2016, 128), BF)],
        (core,),
        (got, sent),
        (near_hidden, start, grad_middle, middle, far_dh),
        scratch=[((864, 128), F32), ((864, 128), F32)],
    )
    other = other_core(other)
    pg1_mine, tokens = call(
        keep_kernel,
        [((1152, 128), F32), ((32, 24, 128), BF)],
        (core,),
        (sent, near_dh),
        (w1, grad_middle),
    )
    (bundle,) = call(
        gather_kernel,
        [((32, ROWS + 24, 128), BF)],
        (),
        (got,),
        (pg1_mine, conv_mine, other, tokens),
        scratch=[((2048, 128), F32)],
    )
    bundle = swap(bundle, CHIPS)
    (spread,) = call(sum_kernel, [((32, ROWS, 128), BF)], (), (bundle,))
    spread = swap(spread, CHIPS)

    rest = bundle[:, ROWS + 16 :]
    rest = jnp.concatenate([rest[:, :, :64], rest[:, :, 64:]], axis=1)
    back = jnp.concatenate([bundle[:, ROWS : ROWS + 16], rest], axis=2).reshape(TOK, CG)
    onehot = (lax.broadcasted_iota(jnp.int32, (TOK, TOK), 0) == (order - base)[None, :]).astype(BF)
    emb_grad = mm(back, onehot, 0, 1).astype(BF)

    out_pg1, out_pg2, out_cg1, out_cg2 = call(
        finish_kernel,
        [((CG, 8 * CG), BF), ((CG, 8 * CG), BF), ((288, 384), BF), ((288, 384), BF)],
        (core,),
        (spread, other_core(spread)),
        scratch=[((2, 32, ROWS, 128), F32), ((CG, 8 * CG), F32)],
        mib=12,
    )
    flat = (1, 3 * CG * CG)
    return emb_grad, out_cg1.reshape(flat), out_pg1, out_cg2.reshape(flat), out_pg2


def solution(mesh):
    fine = Mesh(mesh.devices.reshape(4, 4, 2, 2, 4, 2), SEQ + GRP)
    placed = (P(GRP, SEQ), P(SEQ), P(GRP, SEQ), P(GRP, None), P(GRP, None), P(GRP, None), P(GRP, None))
    return jax.shard_map(
        step,
        mesh=fine,
        in_specs=placed,
        out_specs=(P(GRP, SEQ), P(GRP, None), P(GRP, None), P(GRP, None), P(GRP, None)),
        check_vma=False,
    )
```

```python
import jax
import jax.numpy as jnp
from jax import lax
from jax.experimental import pallas as pl
from jax.experimental.pallas import tpu as pltpu
from jax.sharding import Mesh, PartitionSpec as P

CG = 192
TOK = 512
NEAR = 32
FAR = 64
BF = jnp.bfloat16
F32 = jnp.float32
SEQ = ("zh", "yh", "yl", "core")
GRP = ("x", "zl")
CHIPS = ("zh", "yh", "yl")
SCALE = float(32768) ** (-0.5)
ROWS = 104


def mm(a, b, ca, cb):
    return lax.dot_general(a, b, (((ca,), (cb,)), ((), ())), preferred_element_type=F32)


def swap(blocks, axes):
    return lax.all_to_all(blocks, axes, 0, 0, tiled=True)


def other_core(values):
    return lax.ppermute(values, "core", [(0, 1), (1, 0)])


def call(kernel, outs, scalars, direct, fetched=(), scratch=(), mib=8, space=pl.ANY, flops=0):
    vmem = pl.BlockSpec(memory_space=pltpu.VMEM)
    smem = pl.BlockSpec(memory_space=pltpu.SMEM)
    anywhere = pl.BlockSpec(memory_space=space)
    n_near, n_far, n_out = len(scalars) + len(direct), len(fetched), len(outs)

    def body(*refs):
        near, far, out, rest = (
            refs[:n_near],
            refs[n_near : n_near + n_far],
            refs[n_near + n_far : n_near + n_far + n_out],
            refs[n_near + n_far + n_out :],
        )
        buffers, own = rest[:n_far], rest[n_far:]
        if n_far:
            sems, own = own[-1], own[:-1]
            copies = [pltpu.make_async_copy(far[i], buffers[i], sems.at[i]) for i in range(n_far)]
            for copy in copies:
                copy.start()
            for copy in copies:
                copy.wait()
        kernel(*near, *buffers, *out, *own)

    return pl.pallas_call(
        body,
        out_shape=[jax.ShapeDtypeStruct(shape, dtype) for shape, dtype in outs],
        in_specs=[smem] * len(scalars) + [vmem] * len(direct) + [anywhere] * n_far,
        out_specs=[vmem] * n_out,
        scratch_shapes=[pltpu.VMEM(x.shape, x.dtype) for x in fetched]
        + [pltpu.VMEM(shape, dtype) for shape, dtype in scratch]
        + ([pltpu.SemaphoreType.DMA((n_far,))] if n_far else []),
        compiler_params=pltpu.CompilerParams(vmem_limit_bytes=mib * 1024 * 1024),
        cost_estimate=pl.CostEstimate(flops=flops, bytes_accessed=0, transcendentals=0) if flops else None,
    )(*scalars, *direct, *fetched)


def shifted(values, by):
    if by == 0:
        return values.astype(BF)
    lane = lax.broadcasted_iota(jnp.int32, values.shape, 1)
    rolled = pltpu.roll(values, (-by) % TOK, 1)
    keep = lane < TOK - by if by > 0 else lane >= -by
    return jnp.where(keep, rolled, 0.0).astype(BF)


def conv_back(grads, weight_ref, by):
    return (
        mm(weight_ref[0], shifted(grads, by), 1, 0)
        + mm(weight_ref[1], shifted(grads, 0), 1, 0)
        + mm(weight_ref[2], shifted(grads, -by), 1, 0)
    )


def conv_rows(values, grads, by, rows_ref):
    row = lax.broadcasted_iota(jnp.int32, (CG, CG), 0)
    col = lax.broadcasted_iota(jnp.int32, (CG, CG), 1)
    half = CG // 2
    source = jnp.where(row < half, 2 * row, 2 * row - (CG - 1))
    order = jnp.where(col == source, 1.0, 0.0).astype(BF)
    for tap, distance in enumerate((-by, 0, by)):
        moved = mm(order, shifted(values, distance), 1, 0).astype(BF)
        grad = mm(moved, grads, 1, 1)
        even, odd = grad[:half], grad[half:]
        base = 3 * half * tap
        rows_ref[base : base + half] = even[:, :128]
        rows_ref[base + half : base + 2 * half] = jnp.concatenate([even[:, 128:], odd[:, :64]], axis=1)
        rows_ref[base + 2 * half : base + 3 * half] = odd[:, 64:]


def pack_kernel(base_ref, both_ref, order_ref, out_ref):
    token = lax.broadcasted_iota(jnp.int32, (TOK, TOK), 0)
    onehot = jnp.where(token == order_ref[...] - base_ref[0], 1.0, 0.0).astype(BF)
    start = mm(both_ref[:CG], onehot, 1, 0)
    both = jnp.concatenate([start, both_ref[CG:].astype(F32)], axis=0)
    out_ref[...] = both.T.astype(BF)


def blocks_kernel(weight_ref, out_ref):
    wide = weight_ref[...].astype(F32)
    blank = jnp.zeros((32, 128), F32)
    for j in range(8):
        block = wide[:, CG * j : CG * (j + 1)]
        rest = jnp.concatenate([block[:96, 128:], block[96:, 128:]], axis=1)
        rows = jnp.concatenate([block[:, :128], rest, blank], axis=0)
        for part in range(8):
            out_ref[j, :, 128 * part : 128 * (part + 1)] = rows[40 * part : 40 * (part + 1)].astype(BF)


def near_kernel(tokens_ref, weight_ref, blocks_ref, out_ref, hidden_ref, start_ref):
    rows = tokens_ref[...].astype(F32)
    both = rows.T
    start_ref[...] = both[:CG].astype(BF)
    cot = both[CG:].astype(BF)
    start = rows[:, :CG]
    filler = jnp.zeros((NEAR, CG), F32)
    before = jnp.concatenate([filler, start[: TOK - NEAR]], axis=0).astype(BF)
    after = jnp.concatenate([start[NEAR:], filler], axis=0).astype(BF)
    hidden = (
        mm(weight_ref[0], before, 0, 1)
        + mm(weight_ref[1], start.astype(BF), 0, 1)
        + mm(weight_ref[2], after, 0, 1)
    )
    hidden_ref[...] = hidden
    act = (hidden * jax.nn.sigmoid(hidden)).astype(BF)
    for j in range(8):
        out_ref[j, :CG, :TOK] = act
        out_ref[j, :CG, TOK:] = cot
        out_ref[j, CG:] = blocks_ref[j]


def mid_kernel(
    own_ref, sent_ref, start_ref, pointwise_ref, weight_ref, middle_ref, dh_ref, grad_ref, out_ref, columns_ref
):
    for j in range(8):
        rows = jnp.concatenate(
            [sent_ref[j, CG:, 128 * part : 128 * (part + 1)].astype(F32) for part in range(8)], axis=0
        )
        columns_ref[j, :, :128] = rows[:CG].astype(BF)
        columns_ref[j, :, 128:] = jnp.concatenate([rows[CG:288, :64], rows[CG:288, 64:]], axis=0).astype(BF)
    middle = start_ref[...].astype(F32) + sum(
        mm(pointwise_ref[j * CG : (j + 1) * CG], sent_ref[j, :CG, :TOK], 0, 0) for j in range(8)
    )
    middle = middle.astype(BF)
    middle_ref[...] = middle
    wide = middle.astype(F32)
    hidden = (
        mm(weight_ref[0], shifted(wide, -FAR), 0, 0)
        + mm(weight_ref[1], middle, 0, 0)
        + mm(weight_ref[2], shifted(wide, FAR), 0, 0)
    )
    s = jax.nn.sigmoid(hidden)
    act = (hidden * s).astype(BF)
    blank = jnp.zeros((64, TOK), BF)
    lower = jnp.concatenate([act[128:], blank], axis=0)
    upper = jnp.concatenate([blank, act[128:]], axis=0)
    for j in range(8):
        cot = sent_ref[j, :CG, TOK:]
        rest = mm(cot[:96], lower, 1, 1) + mm(cot[96:], upper, 1, 1)
        rows = jnp.concatenate([mm(cot, act[:128], 1, 1), rest], axis=0)
        for part in range(4):
            out_ref[j, CG:, 128 * part : 128 * (part + 1)] = rows[72 * part : 72 * (part + 1)].astype(BF)
    da = sum(mm(columns_ref[j], sent_ref[j, :CG, TOK:], 0, 0) for j in range(8))
    dh = (da * s * (1.0 + hidden * (1.0 - s))).astype(BF)
    dh_ref[...] = dh
    back = conv_back(dh.astype(F32), weight_ref, FAR)
    grad = (sent_ref[own_ref[0], :CG, TOK:].astype(F32) + back).astype(BF)
    grad_ref[...] = grad
    for j in range(8):
        out_ref[j, :CG] = mm(pointwise_ref[j * CG : (j + 1) * CG], grad, 1, 0).astype(BF)


def block_of(got_ref, core, out_ref, base):
    blank = jnp.zeros((8, 64), F32)
    for j in range(8):
        rows = jnp.concatenate(
            [got_ref[j, CG:, 128 * part : 128 * (part + 1)].astype(F32) for part in range(4)], axis=0
        )
        low = core == 0
        wide = jnp.where(low, rows[:96], rows[96:CG])
        thin = jnp.where(low, rows[CG:, :64], rows[CG:, 64:])
        for part in range(4):
            rest = thin[24 * part : 24 * (part + 1)]
            packed = jnp.concatenate([rest[:8], rest[8:16]], axis=1), jnp.concatenate([rest[16:], blank], axis=1)
            at = base + 160 * j + 40 * part
            piece = jnp.concatenate([wide[24 * part : 24 * (part + 1)], *packed], axis=0)
            out_ref[at : at + 40] = piece.astype(out_ref.dtype)


def columns_of(grad, sent_ref, core, out_ref):
    half = jnp.concatenate([mm(grad, sent_ref[4 * core + j, :CG, :TOK], 1, 1) for j in range(4)], axis=1)
    for j in range(6):
        out_ref[CG * j : CG * (j + 1)] = half[:, 128 * j : 128 * (j + 1)].astype(out_ref.dtype)


def back_kernel(
    core_ref,
    got_ref,
    sent_ref,
    hidden_ref,
    start_ref,
    grad_ref,
    middle_ref,
    far_dh_ref,
    dh_ref,
    mine_ref,
    other_ref,
    far_rows_ref,
    near_rows_ref,
):
    core = core_ref[0]
    da = sum(got_ref[j, :CG].astype(F32) for j in range(8))
    hidden = hidden_ref[...]
    s = jax.nn.sigmoid(hidden)
    dh = (da * s * (1.0 + hidden * (1.0 - s))).astype(BF)
    dh_ref[...] = dh
    conv_rows(start_ref[...].astype(F32), dh, NEAR, near_rows_ref)
    conv_rows(middle_ref[...].astype(F32), far_dh_ref[...], FAR, far_rows_ref)
    mine = pl.ds(pl.multiple_of(432 * core, 8), 432)
    mine_ref[:432] = far_rows_ref[mine]
    mine_ref[432:] = near_rows_ref[mine]
    other = pl.ds(pl.multiple_of(432 - 432 * core, 8), 432)
    other_ref[1152:1584] = far_rows_ref[other].astype(BF)
    other_ref[1584:2016] = near_rows_ref[other].astype(BF)
    block_of(got_ref, 1 - core, other_ref, 2016)
    columns_of(grad_ref[...], sent_ref, 1 - core, other_ref)


def keep_kernel(core_ref, got_ref, sent_ref, dh_ref, weight_ref, grad_ref, mine_ref, out_ref):
    block_of(got_ref, core_ref[0], mine_ref, 1152)
    columns_of(grad_ref[...], sent_ref, core_ref[0], mine_ref)
    back = grad_ref[...].astype(F32) + conv_back(dh_ref[...].astype(F32), weight_ref, NEAR)
    rows = back.T
    out_ref[:, :16] = rows[:, :128].reshape(32, 16, 128).astype(BF)
    rest = rows[:, 128:].reshape(32, 16, 64)
    out_ref[:, 16:] = jnp.concatenate([rest[:, :8], rest[:, 8:]], axis=2).astype(BF)


def gather_kernel(mine_ref, conv_ref, other_ref, tokens_ref, out_ref, rows_ref):
    rows_ref[:1152] = mine_ref[:1152] + other_ref[:1152].astype(F32)
    rows_ref[1152:2016] = conv_ref[...] + other_ref[1152:2016].astype(F32)
    rows_ref[2016:] = jnp.zeros((32, 128), F32)
    out_ref[:, :64] = rows_ref[...].reshape(32, 64, 128).astype(BF)
    rest = mine_ref[1152:] + other_ref[2016:].astype(F32)
    out_ref[:, 64:ROWS] = rest.reshape(32, 40, 128).astype(BF)
    out_ref[:, ROWS:] = tokens_ref[...]


def sum_kernel(got_ref, out_ref):
    total = got_ref[0, :ROWS].astype(F32)
    for j in range(1, 32):
        total = total + got_ref[j, :ROWS].astype(F32)
    piece = (total * SCALE).astype(BF)
    for j in range(32):
        out_ref[j] = piece


def finish_kernel(core_ref, mine_ref, other_ref, near_pw_ref, far_pw_ref, near_conv_ref, far_conv_ref, all_ref, far_ref):
    first = core_ref[0] == 0
    mine = mine_ref[...].astype(F32)
    other = other_ref[...].astype(F32)
    all_ref[0] = jnp.where(first, mine, other)
    all_ref[1] = jnp.where(first, other, mine)
    for j in range(12):
        for part in range(3):
            near_pw_ref[64 * part : 64 * (part + 1), 128 * j : 128 * (j + 1)] = all_ref[
                j // 6, 3 * (j % 6) + part, :64
            ].astype(BF)
    for core in range(2):
        rows = all_ref[core, 18:, :64].reshape(14 * 64, 128)
        for out_ref, at in ((far_conv_ref, 0), (near_conv_ref, 432)):
            for block in range(9):
                place = 9 * core + block
                tap, column, half = place // 6, place // 2 % 3, place % 2
                out_ref[96 * tap + 48 * half : 96 * tap + 48 * (half + 1), 128 * column : 128 * (column + 1)] = rows[
                    at + 48 * block : at + 48 * (block + 1)
                ].astype(BF)
        for part in range(4):
            at = 96 * core + 24 * part
            for pair in range(4):
                blocks = []
                for j in (2 * pair, 2 * pair + 1):
                    piece = all_ref[core, 4 * j + part, 64:ROWS]
                    rest = jnp.concatenate([piece[24:32, :64], piece[24:32, 64:], piece[32:, :64]], axis=0)
                    blocks.append((piece[:24], rest))
                (even, even_rest), (odd, odd_rest) = blocks
                col = 2 * CG * pair
                far_ref[at : at + 24, col : col + 128] = even
                far_ref[at : at + 24, col + 128 : col + 256] = jnp.concatenate([even_rest, odd[:, :64]], axis=1)
                far_ref[at : at + 24, col + 256 : col + 384] = jnp.concatenate([odd[:, 64:], odd_rest], axis=1)
    far_pw_ref[...] = far_ref[...].astype(BF)


def step(emb, order, cot, cw1, pw1, cw2, pw2):
    core = lax.axis_index("core").astype(jnp.int32).reshape(1)
    own = lax.axis_index(GRP).astype(jnp.int32).reshape(1)
    base = (lax.axis_index(SEQ) * TOK).astype(jnp.int32).reshape(1)

    both = jnp.concatenate([emb, cot], axis=0)
    (packed,) = call(pack_kernel, [((TOK, 2 * CG), BF)], (base,), (both,), (order.reshape(1, TOK),))
    packed = swap(packed.reshape(32, TOK // 32, 2 * CG), CHIPS).reshape(TOK, 2 * CG)
    (blocks,) = call(blocks_kernel, [((8, 40, 2 * TOK), BF)], (), (), (pw2,))
    packed, own, core, w1, w2, pw1t, blocks = lax.optimization_barrier(
        (packed, own, core, cw1.reshape(3, CG, CG), cw2.reshape(3, CG, CG), pw1.T, blocks)
    )
    sent, near_hidden, start = call(
        near_kernel,
        [((8, CG + 40, 2 * TOK), BF), ((CG, TOK), F32), ((CG, TOK), BF)],
        (),
        (packed, w1, blocks),
    )
    sent = swap(sent, GRP)
    middle, far_dh, grad_middle, parts = call(
        mid_kernel,
        [((CG, TOK), BF), ((CG, TOK), BF), ((CG, TOK), BF), ((8, CG + 72, TOK), BF)],
        (own,),
        (sent,),
        (start, pw1t, w2),
        scratch=[((8, CG, CG), BF)],
    )
    got = swap(parts, GRP)

    near_dh, conv_mine, other = call(
        back_kernel,
        [((CG, TOK), BF), ((864, 128), F32), ((3296, 128), BF)],
        (core,),
        (got, sent),
        (near_hidden, start, grad_middle, middle, far_dh),
        scratch=[((864, 128), F32), ((864, 128), F32)],
    )
    other = other_core(other)
    mine, tokens = call(
        keep_kernel,
        [((2432, 128), F32), ((32, 24, 128), BF)],
        (core,),
        (got, sent, near_dh),
        (w1, grad_middle),
    )
    (bundle,) = call(
        gather_kernel,
        [((32, ROWS + 24, 128), BF)],
        (),
        (),
        (mine, conv_mine, other, tokens),
        scratch=[((2048, 128), F32)],
    )
    bundle = swap(bundle, CHIPS)
    (spread,) = call(sum_kernel, [((32, ROWS, 128), BF)], (), (bundle,))
    spread = swap(spread, CHIPS)

    rest = bundle[:, ROWS + 16 :]
    rest = jnp.concatenate([rest[:, :, :64], rest[:, :, 64:]], axis=1)
    back = jnp.concatenate([bundle[:, ROWS : ROWS + 16], rest], axis=2).reshape(TOK, CG)
    onehot = (lax.broadcasted_iota(jnp.int32, (TOK, TOK), 0) == (order - base)[None, :]).astype(BF)
    emb_grad = mm(back, onehot, 0, 1).astype(BF)

    out_pg1, out_pg2, out_cg1, out_cg2 = call(
        finish_kernel,
        [((CG, 8 * CG), BF), ((CG, 8 * CG), BF), ((288, 384), BF), ((288, 384), BF)],
        (core,),
        (spread, other_core(spread)),
        scratch=[((2, 32, ROWS, 128), F32), ((CG, 8 * CG), F32)],
        mib=12,
    )
    flat = (1, 3 * CG * CG)
    return emb_grad, out_cg1.reshape(flat), out_pg1, out_cg2.reshape(flat), out_pg2


def solution(mesh):
    fine = Mesh(mesh.devices.reshape(4, 4, 2, 2, 4, 2), SEQ + GRP)
    placed = (P(GRP, SEQ), P(SEQ), P(GRP, SEQ), P(GRP, None), P(GRP, None), P(GRP, None), P(GRP, None))
    return jax.shard_map(
        step,
        mesh=fine,
        in_specs=placed,
        out_specs=(P(GRP, SEQ), P(GRP, None), P(GRP, None), P(GRP, None), P(GRP, None)),
        check_vma=False,
    )
```

```python
import jax
import jax.numpy as jnp
from jax import lax
from jax.experimental import pallas as pl
from jax.experimental.pallas import tpu as pltpu
from jax.sharding import Mesh, PartitionSpec as P

CG = 192
TOK = 512
NEAR = 32
FAR = 64
BF = jnp.bfloat16
F32 = jnp.float32
SEQ = ("zh", "yh", "yl", "core")
GRP = ("x", "zl")
CHIPS = ("zh", "yh", "yl")
SCALE = float(32768) ** (-0.5)
ROWS = 104


def mm(a, b, ca, cb):
    return lax.dot_general(a, b, (((ca,), (cb,)), ((), ())), preferred_element_type=F32)


def swap(blocks, axes):
    return lax.all_to_all(blocks, axes, 0, 0, tiled=True)


def other_core(values):
    return lax.ppermute(values, "core", [(0, 1), (1, 0)])


def call(kernel, outs, scalars, direct, fetched=(), scratch=(), mib=8, space=pl.ANY, flops=0):
    vmem = pl.BlockSpec(memory_space=pltpu.VMEM)
    smem = pl.BlockSpec(memory_space=pltpu.SMEM)
    anywhere = pl.BlockSpec(memory_space=space)
    n_near, n_far, n_out = len(scalars) + len(direct), len(fetched), len(outs)

    def body(*refs):
        near, far, out, rest = (
            refs[:n_near],
            refs[n_near : n_near + n_far],
            refs[n_near + n_far : n_near + n_far + n_out],
            refs[n_near + n_far + n_out :],
        )
        buffers, own = rest[:n_far], rest[n_far:]
        if n_far:
            sems, own = own[-1], own[:-1]
            copies = [pltpu.make_async_copy(far[i], buffers[i], sems.at[i]) for i in range(n_far)]
            for copy in copies:
                copy.start()
            for copy in copies:
                copy.wait()
        kernel(*near, *buffers, *out, *own)

    return pl.pallas_call(
        body,
        out_shape=[jax.ShapeDtypeStruct(shape, dtype) for shape, dtype in outs],
        in_specs=[smem] * len(scalars) + [vmem] * len(direct) + [anywhere] * n_far,
        out_specs=[vmem] * n_out,
        scratch_shapes=[pltpu.VMEM(x.shape, x.dtype) for x in fetched]
        + [pltpu.VMEM(shape, dtype) for shape, dtype in scratch]
        + ([pltpu.SemaphoreType.DMA((n_far,))] if n_far else []),
        compiler_params=pltpu.CompilerParams(vmem_limit_bytes=mib * 1024 * 1024),
        cost_estimate=pl.CostEstimate(flops=flops, bytes_accessed=0, transcendentals=0) if flops else None,
    )(*scalars, *direct, *fetched)


def shifted(values, by):
    if by == 0:
        return values.astype(BF)
    lane = lax.broadcasted_iota(jnp.int32, values.shape, 1)
    rolled = pltpu.roll(values, (-by) % TOK, 1)
    keep = lane < TOK - by if by > 0 else lane >= -by
    return jnp.where(keep, rolled, 0.0).astype(BF)


def conv_back(grads, weight_ref, by):
    return (
        mm(weight_ref[0], shifted(grads, by), 1, 0)
        + mm(weight_ref[1], shifted(grads, 0), 1, 0)
        + mm(weight_ref[2], shifted(grads, -by), 1, 0)
    )


def conv_rows(values, grads, by, rows_ref):
    row = lax.broadcasted_iota(jnp.int32, (CG, CG), 0)
    col = lax.broadcasted_iota(jnp.int32, (CG, CG), 1)
    half = CG // 2
    source = jnp.where(row < half, 2 * row, 2 * row - (CG - 1))
    order = jnp.where(col == source, 1.0, 0.0).astype(BF)
    for tap, distance in enumerate((-by, 0, by)):
        moved = mm(order, shifted(values, distance), 1, 0).astype(BF)
        grad = mm(moved, grads, 1, 1)
        even, odd = grad[:half], grad[half:]
        base = 3 * half * tap
        rows_ref[base : base + half] = even[:, :128]
        rows_ref[base + half : base + 2 * half] = jnp.concatenate([even[:, 128:], odd[:, :64]], axis=1)
        rows_ref[base + 2 * half : base + 3 * half] = odd[:, 64:]


def pack_kernel(base_ref, both_ref, order_ref, out_ref):
    token = lax.broadcasted_iota(jnp.int32, (TOK, TOK), 0)
    onehot = jnp.where(token == order_ref[...] - base_ref[0], 1.0, 0.0).astype(BF)
    start = mm(both_ref[:CG], onehot, 1, 0)
    both = jnp.concatenate([start, both_ref[CG:].astype(F32)], axis=0)
    out_ref[...] = both.T.astype(BF)


def blocks_kernel(weight_ref, out_ref):
    wide = weight_ref[...].astype(F32)
    blank = jnp.zeros((32, 128), F32)
    for j in range(8):
        block = wide[:, CG * j : CG * (j + 1)]
        rest = jnp.concatenate([block[:96, 128:], block[96:, 128:]], axis=1)
        rows = jnp.concatenate([block[:, :128], rest, blank], axis=0)
        for part in range(8):
            out_ref[j, :, 128 * part : 128 * (part + 1)] = rows[40 * part : 40 * (part + 1)].astype(BF)


def near_kernel(tokens_ref, weight_ref, blocks_ref, out_ref, hidden_ref, start_ref):
    rows = tokens_ref[...].astype(F32)
    both = rows.T
    start_ref[...] = both[:CG].astype(BF)
    cot = both[CG:].astype(BF)
    start = rows[:, :CG]
    filler = jnp.zeros((NEAR, CG), F32)
    before = jnp.concatenate([filler, start[: TOK - NEAR]], axis=0).astype(BF)
    after = jnp.concatenate([start[NEAR:], filler], axis=0).astype(BF)
    hidden = (
        mm(weight_ref[0], before, 0, 1)
        + mm(weight_ref[1], start.astype(BF), 0, 1)
        + mm(weight_ref[2], after, 0, 1)
    )
    hidden_ref[...] = hidden
    act = (hidden * jax.nn.sigmoid(hidden)).astype(BF)
    for j in range(8):
        out_ref[j, :CG, :TOK] = act
        out_ref[j, :CG, TOK:] = cot
        out_ref[j, CG:] = blocks_ref[j]


def mid_kernel(
    own_ref, sent_ref, start_ref, pointwise_ref, weight_ref, middle_ref, dh_ref, grad_ref, out_ref, columns_ref
):
    for j in range(8):
        rows = jnp.concatenate(
            [sent_ref[j, CG:, 128 * part : 128 * (part + 1)].astype(F32) for part in range(8)], axis=0
        )
        columns_ref[j, :, :128] = rows[:CG].astype(BF)
        columns_ref[j, :, 128:] = jnp.concatenate([rows[CG:288, :64], rows[CG:288, 64:]], axis=0).astype(BF)
    middle = start_ref[...].astype(F32) + sum(
        mm(pointwise_ref[j * CG : (j + 1) * CG], sent_ref[j, :CG, :TOK], 0, 0) for j in range(8)
    )
    middle = middle.astype(BF)
    middle_ref[...] = middle
    wide = middle.astype(F32)
    hidden = (
        mm(weight_ref[0], shifted(wide, -FAR), 0, 0)
        + mm(weight_ref[1], middle, 0, 0)
        + mm(weight_ref[2], shifted(wide, FAR), 0, 0)
    )
    s = jax.nn.sigmoid(hidden)
    act = (hidden * s).astype(BF)
    blank = jnp.zeros((64, TOK), BF)
    lower = jnp.concatenate([act[128:], blank], axis=0)
    upper = jnp.concatenate([blank, act[128:]], axis=0)
    for j in range(8):
        cot = sent_ref[j, :CG, TOK:]
        rest = mm(cot[:96], lower, 1, 1) + mm(cot[96:], upper, 1, 1)
        rows = jnp.concatenate([mm(cot, act[:128], 1, 1), rest], axis=0)
        for part in range(4):
            out_ref[j, CG:, 128 * part : 128 * (part + 1)] = rows[72 * part : 72 * (part + 1)].astype(BF)
    da = sum(mm(columns_ref[j], sent_ref[j, :CG, TOK:], 0, 0) for j in range(8))
    dh = (da * s * (1.0 + hidden * (1.0 - s))).astype(BF)
    dh_ref[...] = dh
    back = conv_back(dh.astype(F32), weight_ref, FAR)
    grad = (sent_ref[own_ref[0], :CG, TOK:].astype(F32) + back).astype(BF)
    grad_ref[...] = grad
    for j in range(8):
        out_ref[j, :CG] = mm(pointwise_ref[j * CG : (j + 1) * CG], grad, 1, 0).astype(BF)


def block_of(got_ref, core, out_ref, base):
    blank = jnp.zeros((8, 64), F32)
    for j in range(8):
        rows = jnp.concatenate(
            [got_ref[j, CG:, 128 * part : 128 * (part + 1)].astype(F32) for part in range(4)], axis=0
        )
        low = core == 0
        wide = jnp.where(low, rows[:96], rows[96:CG])
        thin = jnp.where(low, rows[CG:, :64], rows[CG:, 64:])
        for part in range(4):
            rest = thin[24 * part : 24 * (part + 1)]
            packed = jnp.concatenate([rest[:8], rest[8:16]], axis=1), jnp.concatenate([rest[16:], blank], axis=1)
            at = base + 160 * j + 40 * part
            piece = jnp.concatenate([wide[24 * part : 24 * (part + 1)], *packed], axis=0)
            out_ref[at : at + 40] = piece.astype(out_ref.dtype)


def columns_of(grad, sent_ref, core, out_ref):
    half = jnp.concatenate([mm(grad, sent_ref[4 * core + j, :CG, :TOK], 1, 1) for j in range(4)], axis=1)
    for j in range(6):
        out_ref[CG * j : CG * (j + 1)] = half[:, 128 * j : 128 * (j + 1)].astype(out_ref.dtype)


def back_kernel(
    core_ref,
    got_ref,
    sent_ref,
    hidden_ref,
    start_ref,
    grad_ref,
    middle_ref,
    far_dh_ref,
    dh_ref,
    mine_ref,
    other_ref,
    far_rows_ref,
    near_rows_ref,
):
    core = core_ref[0]
    da = sum(got_ref[j, :CG].astype(F32) for j in range(8))
    hidden = hidden_ref[...]
    s = jax.nn.sigmoid(hidden)
    dh = (da * s * (1.0 + hidden * (1.0 - s))).astype(BF)
    dh_ref[...] = dh
    conv_rows(start_ref[...].astype(F32), dh, NEAR, near_rows_ref)
    conv_rows(middle_ref[...].astype(F32), far_dh_ref[...], FAR, far_rows_ref)
    mine = pl.ds(pl.multiple_of(432 * core, 8), 432)
    mine_ref[:432] = far_rows_ref[mine]
    mine_ref[432:] = near_rows_ref[mine]
    other = pl.ds(pl.multiple_of(432 - 432 * core, 8), 432)
    other_ref[1152:1584] = far_rows_ref[other].astype(BF)
    other_ref[1584:2016] = near_rows_ref[other].astype(BF)
    block_of(got_ref, 1 - core, other_ref, 2016)
    columns_of(grad_ref[...], sent_ref, 1 - core, other_ref)


def keep_kernel(core_ref, got_ref, sent_ref, dh_ref, weight_ref, grad_ref, mine_ref, out_ref):
    block_of(got_ref, core_ref[0], mine_ref, 1152)
    columns_of(grad_ref[...], sent_ref, core_ref[0], mine_ref)
    back = grad_ref[...].astype(F32) + conv_back(dh_ref[...].astype(F32), weight_ref, NEAR)
    rows = back.T
    out_ref[:, :16] = rows[:, :128].reshape(32, 16, 128).astype(BF)
    rest = rows[:, 128:].reshape(32, 16, 64)
    out_ref[:, 16:] = jnp.concatenate([rest[:, :8], rest[:, 8:]], axis=2).astype(BF)


def gather_kernel(mine_ref, conv_ref, other_ref, tokens_ref, out_ref, rows_ref):
    rows_ref[:1152] = mine_ref[:1152] + other_ref[:1152].astype(F32)
    rows_ref[1152:2016] = conv_ref[...] + other_ref[1152:2016].astype(F32)
    rows_ref[2016:] = jnp.zeros((32, 128), F32)
    out_ref[:, :64] = rows_ref[...].reshape(32, 64, 128).astype(BF)
    rest = mine_ref[1152:] + other_ref[2016:].astype(F32)
    out_ref[:, 64:ROWS] = rest.reshape(32, 40, 128).astype(BF)
    out_ref[:, ROWS:] = tokens_ref[...]


def sum_kernel(got_ref, out_ref):
    total = got_ref[0, :ROWS].astype(F32)
    for j in range(1, 32):
        total = total + got_ref[j, :ROWS].astype(F32)
    piece = (total * SCALE).astype(BF)
    for j in range(32):
        out_ref[j] = piece


def finish_kernel(core_ref, mine_ref, other_ref, near_pw_ref, far_pw_ref, near_conv_ref, far_conv_ref, all_ref, far_ref):
    first = core_ref[0] == 0
    all_ref[0] = jnp.where(first, mine_ref[...], other_ref[...])
    all_ref[1] = jnp.where(first, other_ref[...], mine_ref[...])
    for j in range(12):
        for part in range(3):
            near_pw_ref[64 * part : 64 * (part + 1), 128 * j : 128 * (j + 1)] = all_ref[
                j // 6, 3 * (j % 6) + part, :64
            ].astype(BF)
    for core in range(2):
        rows = all_ref[core, 18:, :64].reshape(14 * 64, 128)
        for out_ref, at in ((far_conv_ref, 0), (near_conv_ref, 432)):
            for block in range(9):
                place = 9 * core + block
                tap, column, half = place // 6, place // 2 % 3, place % 2
                out_ref[96 * tap + 48 * half : 96 * tap + 48 * (half + 1), 128 * column : 128 * (column + 1)] = rows[
                    at + 48 * block : at + 48 * (block + 1)
                ].astype(BF)
        for part in range(4):
            at = 96 * core + 24 * part
            for pair in range(4):
                blocks = []
                for j in (2 * pair, 2 * pair + 1):
                    piece = all_ref[core, 4 * j + part, 64:ROWS].astype(F32)
                    rest = jnp.concatenate([piece[24:32, :64], piece[24:32, 64:], piece[32:, :64]], axis=0)
                    blocks.append((piece[:24], rest))
                (even, even_rest), (odd, odd_rest) = blocks
                col = 2 * CG * pair
                far_ref[at : at + 24, col : col + 128] = even
                far_ref[at : at + 24, col + 128 : col + 256] = jnp.concatenate([even_rest, odd[:, :64]], axis=1)
                far_ref[at : at + 24, col + 256 : col + 384] = jnp.concatenate([odd[:, 64:], odd_rest], axis=1)
    far_pw_ref[...] = far_ref[...].astype(BF)


def step(emb, order, cot, cw1, pw1, cw2, pw2):
    core = lax.axis_index("core").astype(jnp.int32).reshape(1)
    own = lax.axis_index(GRP).astype(jnp.int32).reshape(1)
    base = (lax.axis_index(SEQ) * TOK).astype(jnp.int32).reshape(1)

    both = jnp.concatenate([emb, cot], axis=0)
    (packed,) = call(pack_kernel, [((TOK, 2 * CG), BF)], (base,), (both,), (order.reshape(1, TOK),))
    packed = swap(packed.reshape(32, TOK // 32, 2 * CG), CHIPS).reshape(TOK, 2 * CG)
    (blocks,) = call(blocks_kernel, [((8, 40, 2 * TOK), BF)], (), (), (pw2,))
    packed, own, core, w1, w2, pw1t, blocks = lax.optimization_barrier(
        (packed, own, core, cw1.reshape(3, CG, CG), cw2.reshape(3, CG, CG), pw1.T, blocks)
    )
    sent, near_hidden, start = call(
        near_kernel,
        [((8, CG + 40, 2 * TOK), BF), ((CG, TOK), F32), ((CG, TOK), BF)],
        (),
        (packed, w1, blocks),
    )
    sent = swap(sent, GRP)
    middle, far_dh, grad_middle, parts = call(
        mid_kernel,
        [((CG, TOK), BF), ((CG, TOK), BF), ((CG, TOK), BF), ((8, CG + 72, TOK), BF)],
        (own,),
        (sent,),
        (start, pw1t, w2),
        scratch=[((8, CG, CG), BF)],
    )
    got = swap(parts, GRP)

    near_dh, conv_mine, other = call(
        back_kernel,
        [((CG, TOK), BF), ((864, 128), F32), ((3296, 128), BF)],
        (core,),
        (got, sent),
        (near_hidden, start, grad_middle, middle, far_dh),
        scratch=[((864, 128), F32), ((864, 128), F32)],
    )
    other = other_core(other)
    mine, tokens = call(
        keep_kernel,
        [((2432, 128), F32), ((32, 24, 128), BF)],
        (core,),
        (got, sent, near_dh),
        (w1, grad_middle),
    )
    (bundle,) = call(
        gather_kernel,
        [((32, ROWS + 24, 128), BF)],
        (),
        (),
        (mine, conv_mine, other, tokens),
        scratch=[((2048, 128), F32)],
    )
    bundle = swap(bundle, CHIPS)
    (spread,) = call(sum_kernel, [((32, ROWS, 128), BF)], (), (bundle,))
    spread = swap(spread, CHIPS)

    rest = bundle[:, ROWS + 16 :]
    rest = jnp.concatenate([rest[:, :, :64], rest[:, :, 64:]], axis=1)
    back = jnp.concatenate([bundle[:, ROWS : ROWS + 16], rest], axis=2).reshape(TOK, CG)
    onehot = (lax.broadcasted_iota(jnp.int32, (TOK, TOK), 0) == (order - base)[None, :]).astype(BF)
    emb_grad = mm(back, onehot, 0, 1).astype(BF)

    out_pg1, out_pg2, out_cg1, out_cg2 = call(
        finish_kernel,
        [((CG, 8 * CG), BF), ((CG, 8 * CG), BF), ((288, 384), BF), ((288, 384), BF)],
        (core,),
        (spread, other_core(spread)),
        scratch=[((2, 32, ROWS, 128), BF), ((CG, 8 * CG), F32)],
        mib=12,
    )
    flat = (1, 3 * CG * CG)
    return emb_grad, out_cg1.reshape(flat), out_pg1, out_cg2.reshape(flat), out_pg2


def solution(mesh):
    fine = Mesh(mesh.devices.reshape(4, 4, 2, 2, 4, 2), SEQ + GRP)
    placed = (P(GRP, SEQ), P(SEQ), P(GRP, SEQ), P(GRP, None), P(GRP, None), P(GRP, None), P(GRP, None))
    return jax.shard_map(
        step,
        mesh=fine,
        in_specs=placed,
        out_specs=(P(GRP, SEQ), P(GRP, None), P(GRP, None), P(GRP, None), P(GRP, None)),
        check_vma=False,
    )
```
